32 devices in a mesh: section: 4 (over z), dp: 8 (over y, x, core).
Axes of the slice: x: 2, y: 2, z: 4, core: 2. Of those that a mesh axis runs over, the one named last changes fastest.
Arguments:
- activations: bfloat16 [4, 4, 2048, 1280], P('section', None, 'dp'), may hold values from -6 to 6
- cotangent: bfloat16 [4, 2048, 1280], P(None, 'dp'), may hold values from -1.5 to 1.5
- counts: int32 [4, 8], P(None, 'dp'), may hold values from 64 to 256
- arrival: int32 [4], replicated, may hold values from 0 to 3, each once
- norm_gain: float32 [4, 1280], P('section'), may hold values from 0.1 to 1.9
- qkv_weight: bfloat16 [4, 1280, 1920], P('section'), may hold values from -8 to 8
- out_weight: bfloat16 [4, 1280, 640], P('section'), may hold values from -0.25 to 0.25
Outputs:
- qkv_grad: float32 [4, 1280, 1920], P('section', 'dp')
- out_grad: float32 [4, 1280, 640], P('section', 'dp')
The draws below stay inside these ranges and needn't reach their ends.
Inputs may be any that keep to these rules, and one draw needn't show every extreme that they name: `arrival`: each microbatch once.
All inputs are finite; a program needn't handle non-finite values.
Results may differ from the reference program's by a relative error of at most 0.025.
Values may be sent and summed in bfloat16 or wider, within the bound.
No kernel may reach another device: no remote copies, remote signals or barrier semaphores. Data moves between devices by JAX's collectives and lax.ppermute only.
A program may use at most 128 MiB of HBM per device.

```python
import math
import jax
import jax.numpy as jnp
from jax import lax

D = 1280
HDIM = 80
HEADS = 8
SLOTS = 256
MICRO = 4
LAYERS = 4
HD = 640
QKV = 1920
ROWS = 2048
N_DP = 8


def draw_qkv_weight(key, part):
    base_key = jax.random.fold_in(jax.random.fold_in(key, 11), 0)
    head_span = HEADS * HDIM
    drawn = jax.random.normal(base_key, (LAYERS, D, 3 * head_span), jnp.float32) / math.sqrt(D)
    return jnp.clip(drawn, -8.0, 8.0).astype(jnp.bfloat16)


def touch_ends(entries, stream_key, smallest, largest):
    extent = entries.shape
    spot = [jax.random.randint(jax.random.fold_in(stream_key, axis), (), 0, extent[axis]) for axis in range(len(extent))]
    entries = entries.at[tuple(spot)].set(smallest)
    longest = extent.index(max(extent))
    spot[longest] = (spot[longest] + 1) % extent[longest]
    return entries.at[tuple(spot)].set(largest)


def levels(rng, shape, cuts, least, high):
    gain = 1.0
    for axis_at, blocks in cuts:
        steps = jax.random.uniform(jax.random.fold_in(jax.random.fold_in(rng, 6), axis_at), (blocks,), jnp.float32, least / len(cuts), high / len(cuts))
        gain = gain * jnp.repeat(jnp.exp(steps), shape[axis_at] // blocks).reshape((-1,) + (1,) * (len(shape) - 1 - axis_at))
    return gain


def scatter_about(rng, extent, deviation, most, cuts=(), held_as=jnp.bfloat16):
    factor_of = levels(rng, extent, cuts, -0.22, 0.18) if cuts else 1.0
    values = jax.random.normal(rng, extent, jnp.float32) * deviation * factor_of
    return jnp.minimum(jnp.maximum(values, -most), most).astype(held_as)


def setup_inputs(seed: int = 0) -> dict:
    seeds = jax.random.split(jax.random.key(seed), 8)
    return {
        "activations": scatter_about(seeds[0], (LAYERS, MICRO, ROWS, D), 1.0, 6.0, ((0, 4), (2, 8))),
        "cotangent": scatter_about(seeds[1], (MICRO, ROWS, D), 0.25, 1.5, ((1, 8),)),
        "counts": touch_ends(jax.random.randint(seeds[2], (MICRO, N_DP), SLOTS // 4, SLOTS + 1), jax.random.fold_in(seeds[2], 1), SLOTS // 4, SLOTS).astype(jnp.int32),
        "arrival": jax.random.permutation(seeds[3], MICRO).astype(jnp.int32),
        "norm_gain": jnp.clip(1.0 + 0.18 * jax.random.normal(seeds[4], (LAYERS, D), jnp.float32), 0.1, 1.9),
        "qkv_weight": draw_qkv_weight(jax.random.fold_in(seeds[7], 71), 0),
        "out_weight": scatter_about(seeds[6], (LAYERS, D, HD), HD ** -0.5, 0.25, ((0, 4),)),
    }


EPSILON = 1e-06

def recompute(inputs, visible, gain_row, w_qkv):
    slot_count = inputs.shape[0]
    floats = inputs.astype(jnp.float32)
    centered = floats - lax.optimization_barrier(jnp.mean(floats, axis=-1, keepdims=True))
    inv_std = lax.rsqrt(lax.optimization_barrier(jnp.mean(centered * centered, axis=-1, keepdims=True)) + EPSILON)
    normed = centered * inv_std
    hidden = (normed * gain_row).astype(jnp.bfloat16)
    packed = jnp.dot(hidden, w_qkv, preferred_element_type=jnp.float32).astype(jnp.bfloat16)
    head_span = packed.shape[1] // 3
    queries = packed[:, :head_span].reshape(slot_count, HEADS, HDIM)
    keys_all = packed[:, head_span:2 * head_span].reshape(slot_count, HEADS, HDIM)
    values_all = packed[:, 2 * head_span:].reshape(slot_count, HEADS, HDIM)
    scores = jnp.einsum('ihd,jhd->hij', queries.astype(jnp.float32), keys_all.astype(jnp.float32)) * HDIM ** (-0.5)
    keep = jnp.arange(slot_count) < visible
    scores = jnp.where(keep[None, None, :], scores, -1e+30)
    row_max = lax.optimization_barrier(jnp.max(scores, axis=-1, keepdims=True))
    exp_scores = jnp.exp(scores - row_max)
    prob_full = exp_scores / lax.optimization_barrier(jnp.sum(exp_scores, axis=-1, keepdims=True))
    prob_half = prob_full.astype(jnp.bfloat16)
    attn_out = jnp.einsum('hij,jhd->ihd', prob_half.astype(jnp.float32), values_all.astype(jnp.float32))
    attn_out = attn_out.reshape(slot_count, head_span).astype(jnp.bfloat16)
    return (normed, inv_std, hidden, queries, keys_all, values_all, prob_full, prob_half, attn_out, keep)

def backward_layer(inputs, grad_out, visible, gain_row, w_qkv, w_out):
    slot_count = inputs.shape[0]
    normed, inv_std, hidden, queries, keys_all, values_all, prob_full, prob_half, attn_out, keep = recompute(inputs, visible, gain_row, w_qkv)
    head_span = attn_out.shape[1]
    masked = jnp.where(keep[:, None], grad_out, jnp.zeros_like(grad_out))
    out_part = jnp.dot(masked.T, attn_out, preferred_element_type=jnp.float32)
    grad_attn = jnp.dot(masked, w_out, preferred_element_type=jnp.float32).astype(jnp.bfloat16)
    grad_attn = grad_attn.reshape(slot_count, HEADS, HDIM).astype(jnp.float32)
    grad_prob = jnp.einsum('ihd,jhd->hij', grad_attn, values_all.astype(jnp.float32))
    grad_values = jnp.einsum('hij,ihd->jhd', prob_half.astype(jnp.float32), grad_attn)
    inner = lax.optimization_barrier(jnp.sum(prob_full * grad_prob, axis=-1, keepdims=True))
    grad_scores = (prob_full * (grad_prob - inner) * HDIM ** (-0.5)).astype(jnp.bfloat16).astype(jnp.float32)
    grad_queries = jnp.einsum('hij,jhd->ihd', grad_scores, keys_all.astype(jnp.float32))
    grad_keys = jnp.einsum('hij,ihd->jhd', grad_scores, queries.astype(jnp.float32))
    grad_packed = jnp.concatenate([grad_queries.reshape(slot_count, head_span), grad_keys.reshape(slot_count, head_span), grad_values.reshape(slot_count, head_span)], axis=1).astype(jnp.bfloat16)
    qkv_part = jnp.dot(hidden.T, grad_packed, preferred_element_type=jnp.float32)
    grad_hidden = jnp.dot(grad_packed, w_qkv.T, preferred_element_type=jnp.float32)
    grad_normed = grad_hidden * gain_row
    grad_ln = inv_std * (grad_normed - lax.optimization_barrier(jnp.mean(grad_normed, axis=-1, keepdims=True)) - normed * lax.optimization_barrier(jnp.mean(grad_normed * normed, axis=-1, keepdims=True)))
    grad_in = (masked.astype(jnp.float32) + grad_ln).astype(jnp.bfloat16)
    return (grad_in, qkv_part, out_part)

def reference(activations, cotangent, counts, arrival, norm_gain, qkv_weight, out_weight):
    layer_total = activations.shape[0]
    micro_count = cotangent.shape[0]
    batched = jax.vmap(backward_layer, in_axes=(0, 0, 0, None, None, None))
    flowing = [cotangent[position].reshape(N_DP, SLOTS, D) for position in range(micro_count)]
    qkv_list = []
    out_list = []
    for layer_idx in reversed(range(layer_total)):
        qkv_total = jnp.zeros((D, QKV), jnp.float32)
        out_total = jnp.zeros((D, HD), jnp.float32)
        for position in range(micro_count):
            chosen = arrival[position]
            inputs = activations[layer_idx, chosen].reshape(N_DP, SLOTS, D)
            grad_in, qkv_part, out_part = batched(inputs, flowing[position], counts[chosen], norm_gain[layer_idx], qkv_weight[layer_idx], out_weight[layer_idx])
            qkv_total = qkv_total + lax.optimization_barrier(jnp.sum(qkv_part, axis=0))
            out_total = out_total + lax.optimization_barrier(jnp.sum(out_part, axis=0))
            flowing[position] = grad_in
        qkv_list.insert(0, qkv_total)
        out_list.insert(0, out_total)
    return (jnp.stack(qkv_list), jnp.stack(out_list))
```

```python
import functools

import jax
import jax.numpy as jnp
from jax import lax
from jax.experimental import pallas as pl
from jax.experimental.pallas import tpu as pltpu
from jax.sharding import PartitionSpec as P

HDIM = 80
HEADS = 8
EPSILON = 1e-06
SCALE = HDIM ** (-0.5)
HALF = HEADS // 2
ROWS_AT_A_TIME = 64

BF = jnp.bfloat16
F32 = jnp.float32
VMEM = pl.BlockSpec(memory_space=pltpu.VMEM)
SMEM = pl.BlockSpec(memory_space=pltpu.SMEM)
ANY = pl.BlockSpec(memory_space=pl.ANY)
PARAMS = pltpu.CompilerParams(vmem_limit_bytes=12 << 20)

RECOMPUTED = ("packed", "probs", "normed", "hidden_t", "attn", "inv_std")
COTANGENTS = ("grad_packed", "masked")


def contract(left, right, dims):
    return lax.dot_general(left, right, ((dims[:1], dims[1:]), ((), ())), preferred_element_type=F32)


def head(ref, index, part, h):
    width = HEADS * HDIM
    return ref[index, :, part * width + h * HDIM : part * width + (h + 1) * HDIM]


def recompute_body(position, scalars, x_hbm, gain, w_qkv, *refs):
    packed, probs, normed, hidden_t, attn, inv_std, x_buf, hidden, sem = refs[-9:]
    micro = scalars[2 + position]
    count = scalars[2 + packed.shape[0] + micro]
    copy = pltpu.make_async_copy(x_hbm.at[0, micro], x_buf, sem)
    copy.start()
    copy.wait()
    slots = x_buf.shape[0]
    for start in range(0, slots, ROWS_AT_A_TIME):
        rows = slice(start, start + ROWS_AT_A_TIME)
        floats = x_buf[rows, :].astype(F32)
        centered = floats - jnp.mean(floats, axis=-1, keepdims=True)
        inv = lax.rsqrt(jnp.mean(centered * centered, axis=-1, keepdims=True) + EPSILON)
        unit = centered * inv
        normed[position, rows, :] = unit.astype(BF)
        inv_std[position, rows, :] = jnp.broadcast_to(inv, (ROWS_AT_A_TIME, inv_std.shape[2]))
        hidden[rows, :] = (unit * gain[0:1, :]).astype(BF)
    hidden_t[position] = hidden[...].T
    width = HEADS * HDIM
    for part in range(3):
        cols = slice(part * width, (part + 1) * width)
        packed[position, :, cols] = contract(hidden[...], w_qkv[:, cols], (1, 0)).astype(BF)
    visible = lax.broadcasted_iota(jnp.int32, (slots, slots), 0) < count
    for h in range(HEADS):
        scores = contract(head(packed, position, 1, h), head(packed, position, 0, h), (1, 1)) * SCALE
        scores = jnp.where(visible, scores, -1e30)
        raised = jnp.exp(scores - jnp.max(scores, axis=0, keepdims=True))
        prob = (raised * (1.0 / jnp.sum(raised, axis=0, keepdims=True))).astype(BF)
        probs[position * HEADS + h] = prob
        mixed = contract(head(packed, position, 2, h), prob, (0, 0))
        attn[position, :, h * HDIM : (h + 1) * HDIM] = mixed.T.astype(BF)


def first_body(scalars, x_hbm, gain, wq_hbm, wo_hbm, *refs):
    wq, wo = refs[0], refs[1]
    sem_q, sem_o = refs[-2], refs[-1]
    copy_q = pltpu.make_async_copy(wq_hbm.at[0], wq, sem_q)
    copy_o = pltpu.make_async_copy(wo_hbm.at[0], wo, sem_o)
    copy_q.start()
    copy_o.start()
    copy_q.wait()
    recompute_body(0, scalars, x_hbm, gain, wq, *refs[2:-2])
    copy_o.wait()


def heads_backward(position, heads, first, gattn, packed, probs, out, offsets):
    for h in heads:
        prob = probs[position * HEADS + h]
        g_h = gattn[:, h * HDIM : (h + 1) * HDIM]
        grad_prob = contract(head(packed, position, 2, h), g_h, (1, 1))
        grad_v = contract(prob, g_h, (1, 0))
        full = prob.astype(F32)
        inner = jnp.sum(full * grad_prob, axis=0, keepdims=True)
        grad_s = (full * (grad_prob - inner) * SCALE).astype(BF)
        grad_k = contract(grad_s, head(packed, position, 0, h), (1, 0))
        grad_q = contract(head(packed, position, 1, h), grad_s, (0, 0)).T
        for part, value in enumerate((grad_q, grad_k, grad_v)):
            at = offsets[part] + (h - first) * HDIM
            out[:, at : at + HDIM] = value.astype(BF)


def load_cotangent(is_last, own, arriving, position, g_buf, sem):
    @pl.when(is_last)
    def _():
        copy = pltpu.make_async_copy(own.at[position], g_buf, sem)
        copy.start()
        copy.wait()

    if arriving is not None:

        @pl.when(jnp.logical_not(is_last))
        def _():
            g_buf[...] = arriving[...]


def mask_rows(g_buf, count, masked, position):
    slots = g_buf.shape[0]
    for start in range(0, slots, ROWS_AT_A_TIME):
        rows = slice(start, start + ROWS_AT_A_TIME)
        ids = lax.broadcasted_iota(jnp.int32, (ROWS_AT_A_TIME, g_buf.shape[1]), 0) + start
        kept = jnp.where(ids < count, g_buf[rows, :].astype(F32), 0.0)
        masked[position, rows, :] = kept.astype(BF)


def placing(slot, sections, scalars, micro_count):
    section = scalars[0]
    position = slot - 2 * (sections - 1 - section)
    valid = (position >= 0) & (position < micro_count)
    position = jnp.clip(position, 0, micro_count - 1)
    count = scalars[2 + micro_count + scalars[2 + position]]
    return section, position, valid, count


def backward_body(slot, sections, has_arriving, scalars, own, *refs):
    arriving = None
    if has_arriving:
        arriving, refs = refs[0], refs[1:]
    gain, wq, wo, packed, probs, normed, inv_std = refs[:7]
    passed, grad_packed, masked, g_buf, gattn, sem = refs[-6:]
    section, position, valid, count = placing(slot, sections, scalars, masked.shape[0])

    @pl.when(valid)
    def _():
        load_cotangent(section == sections - 1, own, arriving, position, g_buf, sem)
        mask_rows(g_buf, count, masked, position)
        gattn[...] = contract(masked[position], wo[...], (1, 0)).astype(BF)
        width = HEADS * HDIM
        heads_backward(
            position, range(HEADS), 0, gattn, packed, probs, grad_packed.at[position], (0, width, 2 * width)
        )
        rows_each = 128
        for start in range(0, g_buf.shape[0], rows_each):
            rows = slice(start, start + rows_each)
            grad_normed = contract(grad_packed[position, rows, :], wq[...], (1, 1)) * gain[0:1, :]
            unit = normed[position, rows, :].astype(F32)
            mean = jnp.mean(grad_normed, axis=-1, keepdims=True)
            along = jnp.mean(grad_normed * unit, axis=-1, keepdims=True)
            grad_ln = inv_std[position, rows, 0:1] * (grad_normed - mean - unit * along)
            passed[rows, :] = (masked[position, rows, :].astype(F32) + grad_ln).astype(BF)


def gather_half(source, half, compact):
    width = HEADS * HDIM
    span = HALF * HDIM
    for part in range(3):
        at = part * width + half * span
        compact[:, part * span : (part + 1) * span] = source[:, at : at + span]


def weights_body(index, hidden_t, attn, grad_packed, masked, *refs):
    acc_qkv, acc_out, compact = refs[-3:]
    for half in range(2):
        gather_half(grad_packed.at[index], half, compact)
        total = contract(hidden_t[index], compact[...], (1, 0))
        if index > 0:
            total = total + acc_qkv[half]
        acc_qkv[half] = total
    total = contract(masked[index], attn[index], (0, 0))
    if index > 0:
        total = total + acc_out[...]
    acc_out[...] = total


def blocks_out(dp_index, left, right, acc, sent, kept):
    block = sent.shape[1]
    for j in range(2 * sent.shape[0]):
        at = pl.multiple_of((dp_index ^ j) * block, 16)
        value = contract(left[pl.ds(at, block), :], right, (1, 0))
        if acc is not None:
            value = value + acc[pl.ds(at, block), :]
        target = sent if j % 2 else kept
        target[j // 2] = value.astype(BF)


def tail_out_body(slot, sections, has_arriving, scalars, own, *refs):
    arriving = None
    if has_arriving:
        arriving, refs = refs[0], refs[1:]
    attn, acc_out = refs[:2]
    sent, kept, masked, g_buf, masked_t, sem = refs[-6:]
    section, position, valid, count = placing(slot, sections, scalars, masked.shape[0])
    last = masked.shape[0] - 1

    @pl.when(valid)
    def _():
        load_cotangent(section == sections - 1, own, arriving, position, g_buf, sem)
        mask_rows(g_buf, count, masked, position)

    masked_t[...] = masked[last].T
    blocks_out(scalars[1], masked_t, attn[last], acc_out, sent, kept)


def tail_half_body(slot, sections, half, scalars, wo, packed, probs, masked, hidden_t, acc_qkv, gp_all, *refs):
    sent, kept, gattn, compact = refs[-4:]
    section, position, valid, count = placing(slot, sections, scalars, masked.shape[0])
    last = masked.shape[0] - 1
    span = HALF * HDIM
    width = HEADS * HDIM

    @pl.when(valid)
    def _():
        cols = slice(half * span, (half + 1) * span)
        gattn[:, cols] = contract(masked[position], wo[:, cols], (1, 0)).astype(BF)
        heads_backward(
            position,
            range(half * HALF, (half + 1) * HALF),
            half * HALF,
            gattn,
            packed,
            probs,
            compact,
            (0, span, 2 * span),
        )

    @pl.when(jnp.logical_not(valid))
    def _():
        gather_half(gp_all.at[last], half, compact)

    blocks_out(scalars[1], hidden_t.at[last], compact[...], acc_qkv.at[half], sent, kept)


def halve_body(keeps, sends, kept, arrived, kept_out, sent_out):
    for j, source in enumerate(keeps):
        kept_out[j] = (kept[source].astype(F32) + arrived[source].astype(F32)).astype(BF)
    for j, source in enumerate(sends):
        sent_out[j] = (kept[source].astype(F32) + arrived[source].astype(F32)).astype(BF)


def finish_body(*refs):
    qkv, out = refs[-2:]
    span = HALF * HDIM
    width = HEADS * HDIM
    for half in range(2):
        kept, arrived = refs[2 * half : 2 * half + 2]
        total = kept[0].astype(F32) + arrived[0].astype(F32)
        for part in range(3):
            at = part * width + half * span
            qkv[:, at : at + span] = total[:, part * span : (part + 1) * span]
    cols = out.shape[1] // 2
    for half in range(2):
        kept, arrived = refs[4 + 2 * half : 6 + 2 * half]
        out[:, half * cols : (half + 1) * cols] = kept[0].astype(F32) + arrived[0].astype(F32)


def kept_on_chip(shape, dtype):
    return pltpu.VMEM(shape, dtype)


def per_device(activations, cotangent, counts, arrival, norm_gain, qkv_weight, out_weight):
    sections = lax.axis_size("section")
    dp_count = lax.axis_size("dp")
    section = lax.axis_index("section")
    dp_index = lax.axis_index("dp")
    micro_count, slots, width = cotangent.shape
    packed_width = qkv_weight.shape[2]
    head_width = out_weight.shape[2]
    span = packed_width // 2
    block = width // dp_count
    scalars = jnp.concatenate([jnp.stack([section, dp_index]).astype(jnp.int32), arrival, counts[:, 0]])

    shapes = {
        "packed": kept_on_chip((micro_count, slots, packed_width), BF),
        "probs": kept_on_chip((micro_count * HEADS, slots, slots), BF),
        "normed": kept_on_chip((micro_count, slots, width), BF),
        "hidden_t": kept_on_chip((micro_count, width, slots), BF),
        "attn": kept_on_chip((micro_count, slots, head_width), BF),
        "inv_std": kept_on_chip((micro_count, slots, 128), F32),
        "grad_packed": kept_on_chip((micro_count, slots, packed_width), BF),
        "masked": kept_on_chip((micro_count, slots, width), BF),
    }
    row_scratch = [pltpu.VMEM((slots, width), BF), pltpu.VMEM((slots, width), BF), pltpu.SemaphoreType.DMA]
    state = {}

    def recompute(position, weights):
        outs = tuple(shapes[name] for name in RECOMPUTED)
        if position == 0:
            results = pl.pallas_call(
                first_body,
                out_shape=(
                    kept_on_chip(qkv_weight.shape[1:], BF),
                    kept_on_chip(out_weight.shape[1:], BF),
                    *outs,
                ),
                in_specs=[SMEM, ANY, VMEM, ANY, ANY],
                out_specs=(VMEM,) * (2 + len(outs)),
                scratch_shapes=row_scratch + [pltpu.SemaphoreType.DMA, pltpu.SemaphoreType.DMA],
                compiler_params=PARAMS,
                name="recompute_first",
            )(scalars, activations, norm_gain, qkv_weight, out_weight)
            state.update(zip(RECOMPUTED, results[2:]))
            return results[:2]
        results = pl.pallas_call(
            functools.partial(recompute_body, position),
            out_shape=outs,
            in_specs=[SMEM, ANY, VMEM, VMEM] + [ANY] * len(outs),
            out_specs=(VMEM,) * len(outs),
            scratch_shapes=row_scratch,
            input_output_aliases={4 + i: i for i in range(len(outs))},
            compiler_params=PARAMS,
            name="recompute",
        )(scalars, activations, norm_gain, weights[0], *(state[name] for name in RECOMPUTED))
        state.update(zip(RECOMPUTED, results))
        return weights

    def backward(slot, arriving, weights):
        extra = [] if arriving is None else [arriving]
        outs = (jax.ShapeDtypeStruct((slots, width), BF),) + tuple(shapes[name] for name in COTANGENTS)
        operands = [scalars, cotangent, *extra, norm_gain, *weights]
        operands += [state[name] for name in ("packed", "probs", "normed", "inv_std")]
        specs = [SMEM, ANY] + [VMEM] * (len(operands) - 2)
        aliases = {}
        if "masked" in state:
            aliases = {len(operands) + i: 1 + i for i in range(len(COTANGENTS))}
            operands += [state[name] for name in COTANGENTS]
            specs += [ANY] * len(COTANGENTS)
        results = pl.pallas_call(
            functools.partial(backward_body, slot, sections, arriving is not None),
            out_shape=outs,
            in_specs=specs,
            out_specs=(VMEM,) * len(outs),
            scratch_shapes=[
                pltpu.VMEM((slots, width), BF),
                pltpu.VMEM((slots, head_width), BF),
                pltpu.SemaphoreType.DMA,
            ],
            input_output_aliases=aliases,
            compiler_params=PARAMS,
            name="backward",
        )(*operands)
        state.update(zip(COTANGENTS, results[1:]))
        return results[0]

    def weights_step(index):
        operands = [state[name] for name in ("hidden_t", "attn", "grad_packed", "masked")]
        specs = [VMEM] * len(operands)
        aliases = {}
        if index > 0:
            aliases = {len(operands): 0, len(operands) + 1: 1}
            operands += [state["acc_qkv"], state["acc_out"]]
            specs += [ANY, ANY]
        state["acc_qkv"], state["acc_out"] = pl.pallas_call(
            functools.partial(weights_body, index),
            out_shape=(
                kept_on_chip((2, width, span), F32),
                kept_on_chip((width, head_width), F32),
            ),
            in_specs=specs,
            out_specs=(VMEM, VMEM),
            scratch_shapes=[pltpu.VMEM((slots, span), BF)],
            input_output_aliases=aliases,
            compiler_params=PARAMS,
            name="weights",
        )(*operands)

    def exchange(value, bit):
        pairs = [(source, source ^ bit) for source in range(dp_count)]
        return lax.ppermute(value, "dp", pairs)

    def halve(kept, arrived, bit, held):
        keeps = [i for i, j in enumerate(held) if not j & bit]
        sends = [i for i, j in enumerate(held) if j & bit]
        shape = (len(keeps), *kept.shape[1:])
        kept, sent = pl.pallas_call(
            functools.partial(halve_body, keeps, sends),
            out_shape=(jax.ShapeDtypeStruct(shape, BF), jax.ShapeDtypeStruct(shape, BF)),
            in_specs=[VMEM, VMEM],
            out_specs=(VMEM, VMEM),
            compiler_params=PARAMS,
            name="halve",
        )(kept, arrived)
        return kept, exchange(sent, bit), [held[i] for i in keeps]

    last_slot = micro_count + 2 * (sections - 1) - 1
    in_flight = {}
    weights = None
    for slot in range(last_slot):
        if slot < micro_count:
            weights = recompute(slot, weights)
        passed = backward(slot, in_flight.pop(slot, None), weights)
        pairs = [
            (s, s - 1)
            for s in range(1, sections)
            if 0 <= slot - 2 * (sections - 1 - s) < micro_count
        ]
        if pairs:
            in_flight[slot + 2] = lax.ppermute(passed, "section", pairs)
        index = slot - 2 * (sections - 1)
        if 0 <= index < micro_count - 1:
            weights_step(index)

    arriving = in_flight.pop(last_slot, None)
    extra = [] if arriving is None else [arriving]
    pair_shape = (dp_count // 2, block)
    operands = [scalars, cotangent, *extra, state["attn"], state["acc_out"], state["masked"]]
    sent_out, kept_out, masked = pl.pallas_call(
        functools.partial(tail_out_body, last_slot, sections, arriving is not None),
        out_shape=(
            jax.ShapeDtypeStruct((*pair_shape, head_width), BF),
            jax.ShapeDtypeStruct((*pair_shape, head_width), BF),
            shapes["masked"],
        ),
        in_specs=[SMEM, ANY] + [VMEM] * (len(operands) - 3) + [ANY],
        out_specs=(VMEM,) * 3,
        scratch_shapes=[
            pltpu.VMEM((slots, width), BF),
            pltpu.VMEM((width, slots), BF),
            pltpu.SemaphoreType.DMA,
        ],
        input_output_aliases={len(operands) - 1: 2},
        compiler_params=PARAMS,
        name="tail_out",
    )(*operands)
    arrived_out = exchange(sent_out, 1)

    halves = []
    for half in range(2):
        sent, kept = pl.pallas_call(
            functools.partial(tail_half_body, last_slot, sections, half),
            out_shape=(
                jax.ShapeDtypeStruct((*pair_shape, span), BF),
                jax.ShapeDtypeStruct((*pair_shape, span), BF),
            ),
            in_specs=[SMEM] + [VMEM] * 7,
            out_specs=(VMEM, VMEM),
            scratch_shapes=[pltpu.VMEM((slots, head_width), BF), pltpu.VMEM((slots, span), BF)],
            compiler_params=PARAMS,
            name="tail_qkv",
        )(
            scalars,
            weights[1],
            state["packed"],
            state["probs"],
            masked,
            state["hidden_t"],
            state["acc_qkv"],
            state["grad_packed"],
        )
        halves.append((kept, exchange(sent, 1)))

    bits = [1 << i for i in range(1, dp_count.bit_length() - 1)]
    held = list(range(0, dp_count, 2))
    out_cols = head_width // 2
    streams = [(kept, arrived, held) for kept, arrived in halves]
    streams += [
        (kept_out[:, :, i * out_cols : (i + 1) * out_cols], arrived_out[:, :, i * out_cols : (i + 1) * out_cols], held)
        for i in range(2)
    ]
    orders = [bits, bits[::-1], bits, bits[::-1]]
    for step in range(len(bits)):
        for i in (2, 3, 0, 1):
            kept, arrived, blocks = streams[i]
            streams[i] = halve(kept, arrived, orders[i][step], blocks)
    flat = [x for kept, arrived, _ in streams for x in (kept, arrived)]
    qkv_share, out_share = pl.pallas_call(
        finish_body,
        out_shape=(
            jax.ShapeDtypeStruct((block, packed_width), F32),
            jax.ShapeDtypeStruct((block, head_width), F32),
        ),
        in_specs=[VMEM] * len(flat),
        out_specs=(VMEM, VMEM),
        compiler_params=PARAMS,
        name="finish",
    )(*flat)
    return (qkv_share[None], out_share[None])


def solution(mesh):
    placed = (
        P("section", None, "dp", None),
        P(None, "dp", None),
        P(None, "dp"),
        P(),
        P("section", None),
        P("section", None, None),
        P("section", None, None),
    )
    return jax.shard_map(
        per_device,
        mesh=mesh,
        in_specs=placed,
        out_specs=(P("section", "dp", None), P("section", "dp", None)),
        check_vma=False,
    )
```

```python
import functools

import jax
import jax.numpy as jnp
from jax import lax
from jax.experimental import pallas as pl
from jax.experimental.pallas import tpu as pltpu
from jax.sharding import PartitionSpec as P

HDIM = 80
HEADS = 8
EPSILON = 1e-06
SCALE = HDIM ** (-0.5)
LOG2_E = 1.4426950408889634
HALF = HEADS // 2
ROWS_AT_A_TIME = 128
WIDTH_CHUNKS = 5

BF = jnp.bfloat16
F32 = jnp.float32
VMEM = pl.BlockSpec(memory_space=pltpu.VMEM)
SMEM = pl.BlockSpec(memory_space=pltpu.SMEM)
ANY = pl.BlockSpec(memory_space=pl.ANY)
HBM = pl.BlockSpec(memory_space=pltpu.HBM)
SCRATCH = {
    "recompute_first": 8192,
    "recompute": 6144,
    "backward": 5120,
    "weights": 3072,
    "tail_out": 3072,
    "tail_qkv": 3072,
    "halve_out": 3072,
    "halve": 3072,
    "finish": 3072,
}

RECOMPUTED = ("packed", "values", "probs", "normed", "hidden", "attn", "inv_std", "masked", "inputs")
COTANGENTS = ("grad_packed", "masked")


def contract(left, right, dims=(1, 0)):
    return lax.dot_general(left, right, ((dims[:1], dims[1:]), ((), ())), preferred_element_type=F32)


def head_rows(part, h):
    return pl.ds(pl.multiple_of(part * (HEADS * HDIM) + h * HDIM, 16), HDIM)


def staged(heads, first, second, third):
    first(0, 0)
    first(1, 1)
    second(0, 0)

    def two_steps(i, _):
        h = 2 * i
        third(h, 0)
        second(h + 1, 1)
        first(h + 2, 0)
        third(h + 1, 1)
        second(h + 2, 0)
        first(h + 3, 1)
        return 0

    lax.fori_loop(0, (heads - 2) // 2, two_steps, 0)
    second(heads - 1, 1)
    third(heads - 2, 0)
    third(heads - 1, 1)


def over_lanes(column, lanes):
    return jnp.concatenate([column] * (lanes // column.shape[1]), axis=1)


def normalize(position, x_buf, gain, normed, hidden, inv_std, rows_hidden, unit_rows, inv_rows):
    slots = x_buf.shape[0]

    def some_rows(i, _):
        rows = pl.ds(pl.multiple_of(i * ROWS_AT_A_TIME, ROWS_AT_A_TIME), ROWS_AT_A_TIME)
        floats = x_buf[rows, :].astype(F32)
        centered = floats - jnp.mean(floats, axis=-1, keepdims=True)
        inv = lax.rsqrt(jnp.mean(centered * centered, axis=-1, keepdims=True) + EPSILON)
        unit = centered * inv
        unit_rows[rows, :] = unit.astype(BF)
        inv_rows[rows, :] = jnp.broadcast_to(inv, (ROWS_AT_A_TIME, inv_rows.shape[1]))
        rows_hidden[rows, :] = (unit * gain[0:1, :]).astype(BF)
        return 0

    lax.fori_loop(0, slots // ROWS_AT_A_TIME, some_rows, 0)
    inv_std[position] = inv_rows[...].T[0:8, :]


def project(position, part, w_qkv, packed, values, queries, keys, rows_hidden):
    width = HEADS * HDIM
    got = contract(rows_hidden[...], w_qkv[:, part * width : (part + 1) * width]).astype(BF)
    turned = got.T
    packed[position, part * width : (part + 1) * width, :] = turned
    for h in range(HEADS):
        cols = slice(h * HDIM, (h + 1) * HDIM)
        if part == 0:
            queries[h, 0:HDIM, :] = turned[cols, :]
        if part == 1:
            keys[h, :, 0:HDIM] = got[:, cols]
        if part == 2:
            values[position * HEADS + h] = got[:, cols]


def exclude_keys(count, queries, keys):
    extra = queries.shape[1] - HDIM
    slots = keys.shape[1]
    ones = lax.broadcasted_iota(jnp.int32, (extra, slots), 0) == 0
    ones = jnp.where(ones, 1.0, 0.0).astype(BF)
    past = (lax.broadcasted_iota(jnp.int32, (slots, extra), 0) >= count) & (
        lax.broadcasted_iota(jnp.int32, (slots, extra), 1) == 0
    )
    low = jnp.where(past, -1e30, 0.0).astype(BF)
    for h in range(HEADS):
        queries[h, HDIM:, :] = ones
        keys[h, :, HDIM:] = low


def attend(position, packed, probs, attn, queries, keys, scores, halves):
    def score(h, slot):
        scores[slot][...] = contract(keys[h], queries[h])

    def soften(h, slot):
        raw = scores[slot][...]
        raised = jnp.exp2((raw - jnp.max(raw, axis=0, keepdims=True)) * (SCALE * LOG2_E))
        prob = (raised * (1.0 / jnp.sum(raised, axis=0, keepdims=True))).astype(BF)
        probs[position * HEADS + h] = prob
        halves[slot][...] = prob

    def mix(h, slot):
        attn[position, head_rows(0, h), :] = contract(packed[position, head_rows(2, h), :], halves[slot][...]).astype(BF)

    staged(HEADS, score, soften, mix)


def recompute_body(position, sections, scalars, x_hbm, own, gain, w_qkv, *refs, before_part=None):
    packed, values, probs, normed, hidden, attn, inv_std, masked, inputs = refs[-22:-13]
    rows_hidden, unit_rows, inv_rows, queries, keys, g_buf = refs[-13:-7]
    scores, halves, sems = refs[-7:-5], refs[-5:-3], refs[-3:]
    micro_count = packed.shape[0]
    micro = scalars[2 + position]
    count = scalars[2 + micro_count + micro]
    is_last = scalars[0] == sections - 1
    own_copy = pltpu.make_async_copy(own.at[position], g_buf, sems[1])
    x_buf = inputs.at[position % 2]
    if position == 0:
        copy = pltpu.make_async_copy(x_hbm.at[0, micro], x_buf, sems[0])
        copy.start()
        for part in before_part:
            part.start()
        copy.wait()
    if position + 1 < micro_count:
        following = pltpu.make_async_copy(
            x_hbm.at[0, scalars[3 + position]], inputs.at[(position + 1) % 2], sems[2]
        )
        following.start()

    @pl.when(is_last)
    def _():
        own_copy.start()

    exclude_keys(count, queries, keys)
    normalize(position, x_buf, gain, normed, hidden, inv_std, rows_hidden, unit_rows, inv_rows)
    for part in range(3):
        if before_part is not None:
            before_part[part].wait()
        project(position, part, w_qkv, packed, values, queries, keys, rows_hidden)
        if part == 0:
            normed[position] = unit_rows[...].T
        if part == 1:
            hidden[position] = rows_hidden[...].T
    attend(position, packed, probs, attn, queries, keys, scores, halves)

    @pl.when(is_last)
    def _():
        own_copy.wait()
        turned = g_buf[...].T
        ids = lax.broadcasted_iota(jnp.int32, turned.shape, 1)
        masked[position] = jnp.where(ids < count, turned.astype(F32), 0.0).astype(BF)

    if position + 1 < micro_count:
        following.wait()


def first_body(sections, scalars, x_hbm, own, gain, wq_hbm, wo_hbm, *refs):
    wq, wo_t, gain_t = refs[:3]
    wo, part_sems = refs[-2:]
    width = HEADS * HDIM
    parts = []
    for part in range(3):
        cols = pl.ds(part * width, width)
        parts.append(pltpu.make_async_copy(wq_hbm.at[0, :, cols], wq.at[:, cols], part_sems.at[part]))
    parts.append(pltpu.make_async_copy(wo_hbm.at[0], wo, part_sems.at[3]))
    recompute_body(0, sections, scalars, x_hbm, own, gain, wq, *refs[3:-2], before_part=parts)
    gain_t[...] = jnp.broadcast_to(gain[0:1, :], (gain_t.shape[1], gain.shape[1])).T
    parts[3].wait()
    wo_t[...] = wo[...].T


def heads_backward(position, start, heads, gattn, packed, values, probs, out, offsets, grads, halves):
    def g_rows(h):
        return gattn[pl.ds(pl.multiple_of((start + h) * HDIM, 16), HDIM), :]

    def keep(part, h, value):
        rows = pl.ds(pl.multiple_of(offsets[part] + h * HDIM, 16), HDIM)
        out[rows, :] = value.astype(BF)

    def through_values(h, slot):
        grads[slot][...] = contract(values[position * HEADS + start + h], g_rows(h))

    def through_softmax(h, slot):
        grad_prob = grads[slot][...]
        full = probs[position * HEADS + start + h].astype(F32)
        inner = jnp.sum(full * grad_prob, axis=0, keepdims=True)
        halves[slot][...] = (full * (grad_prob - inner)).astype(BF)

    def through_scores(h, slot):
        grad_s = halves[slot][...]
        keep(0, h, contract(packed[position, head_rows(1, start + h), :], grad_s) * SCALE)
        keep(1, h, contract(packed[position, head_rows(0, start + h), :], grad_s, (1, 1)) * SCALE)
        keep(2, h, contract(g_rows(h), probs[position * HEADS + start + h], (1, 1)))

    staged(heads, through_values, through_softmax, through_scores)


def placing(slot, sections, scalars, micro_count):
    section = scalars[0]
    position = slot - 2 * (sections - 1 - section)
    valid = (position >= 0) & (position < micro_count)
    position = jnp.clip(position, 0, micro_count - 1)
    count = scalars[2 + micro_count + scalars[2 + position]]
    return section, position, valid, count


def take_arriving(sections, section, arriving, position, masked):
    if arriving is not None:

        @pl.when(section != sections - 1)
        def _():
            masked[position] = arriving[...]


def backward_body(slot, sections, has_arriving, passes, scalars, *refs):
    arriving = None
    if has_arriving:
        arriving, refs = refs[0], refs[1:]
    wq, wo_t, gain_t, packed, values, probs, normed, inv_std = refs[:8]
    if passes:
        passed, refs = refs[-9], (*refs[:-9], *refs[-8:])
    grad_packed, masked, gattn, grad_hidden = refs[-8:-4]
    grads, halves = refs[-4:-2], refs[-2:]
    section, position, valid, count = placing(slot, sections, scalars, masked.shape[0])
    width, slots = masked.shape[1:]

    @pl.when(valid)
    def _():
        take_arriving(sections, section, arriving, position, masked)
        gattn[...] = contract(wo_t[...], masked[position]).astype(BF)
        span = HEADS * HDIM
        heads_backward(
            position,
            0,
            HEADS,
            gattn,
            packed,
            values,
            probs,
            grad_packed.at[position],
            (0, span, 2 * span),
            grads,
            halves,
        )

    if not passes:
        return

    @pl.when(valid & (section > 0))
    def _():
        chunk = width // WIDTH_CHUNKS

        def some_width(i, carry):
            total, along = carry
            rows = pl.ds(pl.multiple_of(i * chunk, 16), chunk)
            got = contract(wq[rows, :], grad_packed[position]) * over_lanes(gain_t[rows, :], slots)
            grad_hidden[rows, :] = got
            unit = normed[position, rows, :].astype(F32)
            total = total + jnp.sum(got, axis=0, keepdims=True)
            along = along + jnp.sum(got * unit, axis=0, keepdims=True)
            return total, along

        zero = jnp.zeros((1, slots), F32)
        total, along = lax.fori_loop(0, WIDTH_CHUNKS, some_width, (zero, zero))
        mean = total * (1.0 / width)
        along = along * (1.0 / width)
        shown = lax.broadcasted_iota(jnp.int32, (1, slots), 1) < count
        inv = jnp.where(shown, inv_std[position, 0:1, :], 0.0)

        def finish(i, _):
            rows = pl.ds(pl.multiple_of(i * chunk, 16), chunk)
            unit = normed[position, rows, :].astype(F32)
            grad_ln = inv * (grad_hidden[rows, :] - mean - unit * along)
            passed[rows, :] = (masked[position, rows, :].astype(F32) + grad_ln).astype(BF)
            return 0

        lax.fori_loop(0, WIDTH_CHUNKS, finish, 0)


def gather_half(source, half, compact):
    width = HEADS * HDIM
    span = HALF * HDIM
    for part in range(3):
        at = part * width + half * span
        compact[part * span : (part + 1) * span, :] = source[at : at + span, :]


def weights_body(index, hidden, attn, grad_packed, masked, *refs):
    acc_out, compact = refs[-2:]
    acc_qkv = refs[-4:-2]
    width = hidden.shape[1]
    chunk = width // 5

    def some_width(i, _):
        rows = pl.ds(pl.multiple_of(i * chunk, 16), chunk)
        for half in range(2):
            total = contract(hidden[index, rows, :], compact[half], (1, 1))
            if index > 0:
                total = total + acc_qkv[half][rows, :].astype(F32)
            acc_qkv[half][rows, :] = total.astype(BF)
        total = contract(masked[index, rows, :], attn[index], (1, 1))
        if index > 0:
            total = total + acc_out[rows, :].astype(F32)
        acc_out[rows, :] = total.astype(BF)
        return 0

    for half in range(2):
        gather_half(grad_packed.at[index], half, compact.at[half])
    lax.fori_loop(0, 5, some_width, 0)


def blocks_out(dp_index, left, right, acc, sent, kept):
    count, block = sent.shape[:2]

    def one(j, target, to):
        at = pl.multiple_of((dp_index ^ j) * block, 16)
        value = contract(left[pl.ds(at, block), :], right, (1, 1)) + acc[pl.ds(at, block), :].astype(F32)
        target[to] = value.astype(BF)

    def two(i, _):
        one(2 * i + 1, sent, i)
        one(2 * i, kept, i)
        return 0

    lax.fori_loop(0, count, two, 0)


def tail_out_body(slot, sections, has_arriving, scalars, *refs):
    arriving = None
    if has_arriving:
        arriving, refs = refs[0], refs[1:]
    attn, acc_out = refs[:2]
    sent, kept, masked = refs[-3:]
    section, position, valid, _ = placing(slot, sections, scalars, masked.shape[0])
    last = masked.shape[0] - 1

    @pl.when(valid)
    def _():
        take_arriving(sections, section, arriving, position, masked)

    blocks_out(scalars[1], masked.at[last], attn[last], acc_out, sent, kept)


def tail_half_body(slot, sections, half, scalars, wo_t, packed, values, probs, masked, hidden, acc_qkv, gp_all, *refs):
    sent, kept, gattn, compact = refs[-8:-4]
    grads, halves = refs[-4:-2], refs[-2:]
    _, position, valid, _ = placing(slot, sections, scalars, masked.shape[0])
    last = masked.shape[0] - 1
    span = HALF * HDIM

    @pl.when(valid)
    def _():
        rows = slice(half * span, (half + 1) * span)
        gattn[rows, :] = contract(wo_t[rows, :], masked[position]).astype(BF)
        heads_backward(
            position,
            half * HALF,
            HALF,
            gattn,
            packed,
            values,
            probs,
            compact,
            (0, span, 2 * span),
            grads,
            halves,
        )

    @pl.when(jnp.logical_not(valid))
    def _():
        gather_half(gp_all.at[last], half, compact)

    blocks_out(scalars[1], hidden.at[last], compact[...], acc_qkv, sent, kept)


def halve_out_body(split, keeps, sends, kept, arrived, *outs):
    for piece, cols in enumerate((slice(0, split), slice(split, kept.shape[2]))):
        kept_out, sent_out = outs[2 * piece : 2 * piece + 2]
        for target, sources in ((kept_out, keeps[piece]), (sent_out, sends[piece])):
            for j, source in enumerate(sources):
                target[j] = (kept[source, :, cols].astype(F32) + arrived[source, :, cols].astype(F32)).astype(BF)


def halve_body(keeps, sends, kept, arrived, kept_out, sent_out):
    for j, source in enumerate(keeps):
        kept_out[j] = (kept[source].astype(F32) + arrived[source].astype(F32)).astype(BF)
    for j, source in enumerate(sends):
        sent_out[j] = (kept[source].astype(F32) + arrived[source].astype(F32)).astype(BF)


def finish_body(split, *refs):
    qkv, out = refs[-2:]
    span = HALF * HDIM
    width = HEADS * HDIM
    for half in range(2):
        kept, arrived = refs[2 * half : 2 * half + 2]
        total = kept[0].astype(F32) + arrived[0].astype(F32)
        for part in range(3):
            at = part * width + half * span
            qkv[:, at : at + span] = total[:, part * span : (part + 1) * span]
    for piece, cols in enumerate((slice(0, split), slice(split, out.shape[1]))):
        kept, arrived = refs[4 + 2 * piece : 6 + 2 * piece]
        out[:, cols] = kept[0].astype(F32) + arrived[0].astype(F32)


def kept_on_chip(shape, dtype):
    return pltpu.VMEM(shape, dtype)


def per_device(activations, cotangent, counts, arrival, norm_gain, qkv_weight, out_weight):
    sections = lax.axis_size("section")
    dp_count = lax.axis_size("dp")
    section = lax.axis_index("section")
    dp_index = lax.axis_index("dp")
    micro_count, slots, width = cotangent.shape
    packed_width = qkv_weight.shape[2]
    head_width = out_weight.shape[2]
    span = packed_width // 2
    block = width // dp_count
    activations, cotangent, qkv_weight, out_weight = (
        pltpu.with_memory_space_constraint(x, pltpu.HBM)
        for x in (activations, cotangent, qkv_weight, out_weight)
    )
    scalars = jnp.concatenate([jnp.stack([section, dp_index]).astype(jnp.int32), arrival, counts[:, 0]])

    shapes = {
        "packed": kept_on_chip((micro_count, packed_width, slots), BF),
        "values": kept_on_chip((micro_count * HEADS, slots, HDIM), BF),
        "probs": kept_on_chip((micro_count * HEADS, slots, slots), BF),
        "normed": kept_on_chip((micro_count, width, slots), BF),
        "hidden": kept_on_chip((micro_count, width, slots), BF),
        "attn": kept_on_chip((micro_count, head_width, slots), BF),
        "inv_std": kept_on_chip((micro_count, 8, slots), F32),
        "grad_packed": kept_on_chip((micro_count, packed_width, slots), BF),
        "inputs": kept_on_chip((2, slots, width), BF),
        "masked": kept_on_chip((micro_count, width, slots), BF),
    }
    head_scratch = [pltpu.VMEM((slots, slots), F32)] * 2 + [pltpu.VMEM((slots, slots), BF)] * 2
    row_scratch = [
        pltpu.VMEM((slots, width), BF),
        pltpu.VMEM((slots, width), BF),
        pltpu.VMEM((slots, 128), F32),
        pltpu.VMEM((HEADS, HDIM + 16, slots), BF),
        pltpu.VMEM((HEADS, slots, HDIM + 16), BF),
        pltpu.VMEM((slots, width), BF),
        *head_scratch,
        pltpu.SemaphoreType.DMA,
        pltpu.SemaphoreType.DMA,
        pltpu.SemaphoreType.DMA,
    ]
    state = {}

    def recompute(position, weights):
        outs = tuple(shapes[name] for name in RECOMPUTED)
        if position == 0:
            results = pl.pallas_call(
                functools.partial(first_body, sections),
                out_shape=(
                    kept_on_chip(qkv_weight.shape[1:], BF),
                    kept_on_chip((head_width, width), BF),
                    kept_on_chip((width, 128), F32),
                    *outs,
                ),
                in_specs=[SMEM, HBM, HBM, VMEM, HBM, HBM],
                out_specs=(VMEM,) * (3 + len(outs)),
                scratch_shapes=row_scratch + [pltpu.VMEM((width, head_width), BF), pltpu.SemaphoreType.DMA((4,))],
                compiler_params=pltpu.CompilerParams(vmem_limit_bytes=SCRATCH["recompute_first"] << 10),
                name="recompute_first",
            )(scalars, activations, cotangent, norm_gain, qkv_weight, out_weight)
            state.update(zip(RECOMPUTED, results[3:]))
            return results[:3]
        results = pl.pallas_call(
            functools.partial(recompute_body, position, sections),
            out_shape=outs,
            in_specs=[SMEM, HBM, HBM, VMEM, VMEM] + [ANY] * len(outs),
            out_specs=(VMEM,) * len(outs),
            scratch_shapes=row_scratch,
            input_output_aliases={5 + i: i for i in range(len(outs))},
            compiler_params=pltpu.CompilerParams(vmem_limit_bytes=SCRATCH["recompute"] << 10),
            name="recompute",
        )(scalars, activations, cotangent, norm_gain, weights[0], *(state[name] for name in RECOMPUTED))
        state.update(zip(RECOMPUTED, results))
        return weights

    def backward(slot, arriving, weights, passes):
        extra = [] if arriving is None else [arriving]
        outs = tuple(shapes[name] for name in COTANGENTS)
        if passes:
            outs = (jax.ShapeDtypeStruct((width, slots), BF), *outs)
        operands = [scalars, *extra, *weights]
        operands += [state[name] for name in ("packed", "values", "probs", "normed", "inv_std")]
        specs = [SMEM] + [VMEM] * (len(operands) - 1)
        given = [name for name in COTANGENTS if name in state]
        aliases = {len(operands) + i: passes + COTANGENTS.index(name) for i, name in enumerate(given)}
        operands += [state[name] for name in given]
        specs += [ANY] * len(given)
        results = pl.pallas_call(
            functools.partial(backward_body, slot, sections, arriving is not None, passes),
            out_shape=outs,
            in_specs=specs,
            out_specs=(VMEM,) * len(outs),
            scratch_shapes=[
                pltpu.VMEM((head_width, slots), BF),
                pltpu.VMEM((width, slots), F32),
                *head_scratch,
            ],
            input_output_aliases=aliases,
            compiler_params=pltpu.CompilerParams(vmem_limit_bytes=SCRATCH["backward"] << 10),
            name="backward",
        )(*operands)
        state.update(zip(COTANGENTS, results[-2:]))
        return results[0]

    def weights_step(index):
        operands = [state[name] for name in ("hidden", "attn", "grad_packed", "masked")]
        specs = [VMEM] * len(operands)
        aliases = {}
        if index > 0:
            aliases = {len(operands) + i: i for i in range(3)}
            operands += state["sums"]
            specs += [ANY] * 3
        state["sums"] = pl.pallas_call(
            functools.partial(weights_body, index),
            out_shape=(
                kept_on_chip((width, span), BF),
                kept_on_chip((width, span), BF),
                kept_on_chip((width, head_width), BF),
            ),
            in_specs=specs,
            out_specs=(VMEM,) * 3,
            scratch_shapes=[pltpu.VMEM((2, span, slots), BF)],
            input_output_aliases=aliases,
            compiler_params=pltpu.CompilerParams(vmem_limit_bytes=SCRATCH["weights"] << 10),
            name="weights",
        )(*operands)

    def exchange(value, bit):
        pairs = [(source, source ^ bit) for source in range(dp_count)]
        return lax.ppermute(value, "dp", pairs)

    def halve(kept, arrived, bit, held):
        keeps = [i for i, j in enumerate(held) if not j & bit]
        sends = [i for i, j in enumerate(held) if j & bit]
        shape = (len(keeps), *kept.shape[1:])
        kept, sent = pl.pallas_call(
            functools.partial(halve_body, keeps, sends),
            out_shape=(jax.ShapeDtypeStruct(shape, BF), jax.ShapeDtypeStruct(shape, BF)),
            in_specs=[VMEM, VMEM],
            out_specs=(VMEM, VMEM),
            compiler_params=pltpu.CompilerParams(vmem_limit_bytes=SCRATCH["halve"] << 10),
            name="halve",
        )(kept, arrived)
        return kept, exchange(sent, bit), [held[i] for i in keeps]

    last_slot = micro_count + 2 * (sections - 1) - 1
    in_flight = {}
    weights = None
    for slot in range(last_slot):
        if slot < micro_count:
            weights = recompute(slot, weights)
        pairs = [
            (s, s - 1)
            for s in range(1, sections)
            if 0 <= slot - 2 * (sections - 1 - s) < micro_count
        ]
        passed = backward(slot, in_flight.pop(slot, None), weights, bool(pairs))
        if pairs:
            in_flight[slot + 2] = lax.ppermute(passed, "section", pairs)
        index = slot - 2 * (sections - 1)
        if 0 <= index < micro_count - 1:
            weights_step(index)

    arriving = in_flight.pop(last_slot, None)
    extra = [] if arriving is None else [arriving]
    pair_shape = (dp_count // 2, block)
    operands = [scalars, *extra, state["attn"], state["sums"][2], state["masked"]]
    sent_out, kept_out, masked = pl.pallas_call(
        functools.partial(tail_out_body, last_slot, sections, arriving is not None),
        out_shape=(
            jax.ShapeDtypeStruct((*pair_shape, head_width), BF),
            jax.ShapeDtypeStruct((*pair_shape, head_width), BF),
            shapes["masked"],
        ),
        in_specs=[SMEM] + [VMEM] * (len(operands) - 2) + [ANY],
        out_specs=(VMEM,) * 3,
        input_output_aliases={len(operands) - 1: 2},
        compiler_params=pltpu.CompilerParams(vmem_limit_bytes=SCRATCH["tail_out"] << 10),
        name="tail_out",
    )(*operands)
    arrived_out = exchange(sent_out, 1)

    def tail_half(half, scalars):
        sent, kept = pl.pallas_call(
            functools.partial(tail_half_body, last_slot, sections, half),
            out_shape=(
                jax.ShapeDtypeStruct((*pair_shape, span), BF),
                jax.ShapeDtypeStruct((*pair_shape, span), BF),
            ),
            in_specs=[SMEM] + [VMEM] * 8,
            out_specs=(VMEM, VMEM),
            scratch_shapes=[pltpu.VMEM((head_width, slots), BF), pltpu.VMEM((span, slots), BF), *head_scratch],
            compiler_params=pltpu.CompilerParams(vmem_limit_bytes=SCRATCH["tail_qkv"] << 10),
            name="tail_qkv",
        )(
            scalars,
            weights[1],
            state["packed"],
            state["values"],
            state["probs"],
            masked,
            state["hidden"],
            state["sums"][half],
            state["grad_packed"],
        )
        return kept, exchange(sent, 1)

    bits = [1 << i for i in range(1, dp_count.bit_length() - 1)]
    held = list(range(0, dp_count, 2))
    split = head_width // 256 * 128
    first = tail_half(0, scalars)
    keeps = [[i for i, j in enumerate(held) if not j & bit] for bit in (bits[0], bits[-1])]
    sends = [[i for i, j in enumerate(held) if j & bit] for bit in (bits[0], bits[-1])]
    piece_shapes = [
        jax.ShapeDtypeStruct((len(held) // 2, block, cols), BF)
        for cols in (split, split, head_width - split, head_width - split)
    ]
    kept_a, sent_a, kept_b, sent_b = pl.pallas_call(
        functools.partial(halve_out_body, split, keeps, sends),
        out_shape=tuple(piece_shapes),
        in_specs=[VMEM, VMEM],
        out_specs=(VMEM,) * 4,
        compiler_params=pltpu.CompilerParams(vmem_limit_bytes=SCRATCH["halve_out"] << 10),
        name="halve_out",
    )(kept_out, arrived_out)
    later_scalars, kept_a, sent_a, kept_b, sent_b = lax.optimization_barrier(
        (scalars, kept_a, sent_a, kept_b, sent_b)
    )
    out_streams = [
        (kept_a, exchange(sent_a, bits[0]), [held[i] for i in keeps[0]]),
        (kept_b, exchange(sent_b, bits[-1]), [held[i] for i in keeps[1]]),
    ]
    second = tail_half(1, later_scalars)
    orders = [bits, bits[::-1]]
    qkv_streams = [(*first, held), (*second, held)]
    for step in range(len(bits)):
        if step > 0:
            for i in range(2):
                out_streams[i] = halve(*out_streams[i][:2], orders[i][step], out_streams[i][2])
        for i in range(2):
            qkv_streams[i] = halve(*qkv_streams[i][:2], orders[i][step], qkv_streams[i][2])
    flat = [x for kept, arrived, _ in qkv_streams + out_streams for x in (kept, arrived)]
    qkv_share, out_share = pl.pallas_call(
        functools.partial(finish_body, split),
        out_shape=(
            jax.ShapeDtypeStruct((block, packed_width), F32),
            jax.ShapeDtypeStruct((block, head_width), F32),
        ),
        in_specs=[VMEM] * len(flat),
        out_specs=(VMEM, VMEM),
        compiler_params=pltpu.CompilerParams(vmem_limit_bytes=SCRATCH["finish"] << 10),
        name="finish",
    )(*flat)
    return (qkv_share[None], out_share[None])


def solution(mesh):
    placed = (
        P("section", None, "dp", None),
        P(None, "dp", None),
        P(None, "dp"),
        P(),
        P("section", None),
        P("section", None, None),
        P("section", None, None),
    )
    return jax.shard_map(
        per_device,
        mesh=mesh,
        in_specs=placed,
        out_specs=(P("section", "dp", None), P("section", "dp", None)),
        check_vma=False,
    )
```

```python
import functools

import jax
import jax.numpy as jnp
from jax import lax
from jax.experimental import pallas as pl
from jax.experimental.pallas import tpu as pltpu
from jax.sharding import PartitionSpec as P


HDIM = 80
HEADS = 8
EPSILON = 1e-06
SCALE = HDIM ** (-0.5)
LOG2_E = 1.4426950408889634
PIECES = (HEADS // 2 + 1, HEADS // 2 - 1)
ROWS_AT_A_TIME = 128
WIDTH_CHUNKS = 5

BF = jnp.bfloat16
F32 = jnp.float32
VMEM = pl.BlockSpec(memory_space=pltpu.VMEM)
SMEM = pl.BlockSpec(memory_space=pltpu.SMEM)
ANY = pl.BlockSpec(memory_space=pl.ANY)
HBM = pl.BlockSpec(memory_space=pltpu.HBM)
SCRATCH = {
    "recompute_first": 8192,
    "recompute": 6144,
    "backward": 5120,
    "weights": 3072,
    "tail_out": 3072,
    "tail_qkv": 3072,
    "halve_out": 3072,
    "halve": 3072,
    "finish": 3072,
}

RECOMPUTED = ("packed", "values", "probs", "normed", "hidden", "attn", "inv_std", "masked", "inputs")
COTANGENTS = ("grad_packed", "masked")


def contract(left, right, dims=(1, 0)):
    return lax.dot_general(left, right, ((dims[:1], dims[1:]), ((), ())), preferred_element_type=F32)


def head_rows(part, h):
    return pl.ds(pl.multiple_of(part * (HEADS * HDIM) + h * HDIM, 16), HDIM)


def staged(heads, first, second, third):
    first(0, 0)
    first(1, 1)
    second(0, 0)

    def two_steps(i, _):
        h = 2 * i
        third(h, 0)
        second(h + 1, 1)
        first(h + 2, 0)
        third(h + 1, 1)
        second(h + 2, 0)
        first(h + 3, 1)
        return 0

    lax.fori_loop(0, (heads - 2) // 2, two_steps, 0)
    final = heads - 1
    if heads % 2:
        third(final - 2, 0)
        second(final - 1, 1)
        first(final, 0)
    second(final, final % 2)
    third(final - 1, 1 - final % 2)
    third(final, final % 2)


def over_lanes(column, lanes):
    return jnp.concatenate([column] * (lanes // column.shape[1]), axis=1)


def normalize(position, x_buf, gain, inv_std, rows_hidden, unit_rows, inv_rows):
    slots = x_buf.shape[0]

    def some_rows(i, _):
        rows = pl.ds(pl.multiple_of(i * ROWS_AT_A_TIME, ROWS_AT_A_TIME), ROWS_AT_A_TIME)
        floats = x_buf[rows, :].astype(F32)
        centered = floats - jnp.mean(floats, axis=-1, keepdims=True)
        inv = lax.rsqrt(jnp.mean(centered * centered, axis=-1, keepdims=True) + EPSILON)
        unit = centered * inv
        unit_rows[rows, :] = unit.astype(BF)
        inv_rows[rows, :] = jnp.broadcast_to(inv, (ROWS_AT_A_TIME, inv_rows.shape[1]))
        rows_hidden[rows, :] = (unit * gain[0:1, :]).astype(BF)
        return 0

    lax.fori_loop(0, slots // ROWS_AT_A_TIME, some_rows, 0)
    inv_std[position] = inv_rows[...].T[0:8, :]


def project(position, part, w_qkv, packed, values, queries, keys, rows_hidden):
    width = HEADS * HDIM
    got = contract(rows_hidden[...], w_qkv[:, part * width : (part + 1) * width]).astype(BF)
    turned = got.T
    packed[position, part * width : (part + 1) * width, :] = turned
    for h in range(HEADS):
        cols = slice(h * HDIM, (h + 1) * HDIM)
        if part == 0:
            queries[h, 0:HDIM, :] = turned[cols, :]
        if part == 1:
            keys[h, :, 0:HDIM] = got[:, cols]
        if part == 2:
            values[position * HEADS + h] = got[:, cols]


def exclude_keys(count, queries, keys):
    extra = queries.shape[1] - HDIM
    slots = keys.shape[1]
    ones = lax.broadcasted_iota(jnp.int32, (extra, slots), 0) == 0
    ones = jnp.where(ones, 1.0, 0.0).astype(BF)
    past = (lax.broadcasted_iota(jnp.int32, (slots, extra), 0) >= count) & (
        lax.broadcasted_iota(jnp.int32, (slots, extra), 1) == 0
    )
    low = jnp.where(past, -1e30, 0.0).astype(BF)
    for h in range(HEADS):
        queries[h, HDIM:, :] = ones
        keys[h, :, HDIM:] = low


def attend(position, packed, probs, attn, queries, keys, scores, halves):
    def score(h, slot):
        scores[slot][...] = contract(keys[h], queries[h])

    def soften(h, slot):
        raw = scores[slot][...]
        raised = jnp.exp2((raw - jnp.max(raw, axis=0, keepdims=True)) * (SCALE * LOG2_E))
        prob = (raised * (1.0 / jnp.sum(raised, axis=0, keepdims=True))).astype(BF)
        probs[position * HEADS + h] = prob
        halves[slot][...] = prob

    def mix(h, slot):
        attn[position, head_rows(0, h), :] = contract(packed[position, head_rows(2, h), :], halves[slot][...]).astype(BF)

    staged(HEADS, score, soften, mix)


def recompute_at(position, sections, scalars, x_hbm, own, gain, w_qkv, refs, before_part=None):
    packed, values, probs, normed, hidden, attn, inv_std, masked, inputs = refs[-22:-13]
    rows_hidden, unit_rows, inv_rows, queries, keys, g_buf = refs[-13:-7]
    scores, halves, sems = refs[-7:-5], refs[-5:-3], refs[-3:]
    micro_count = packed.shape[0]
    micro = scalars[2 + position]
    count = scalars[2 + micro_count + micro]
    is_last = scalars[0] == sections - 1
    own_copy = pltpu.make_async_copy(own.at[position], g_buf, sems[1])
    x_buf = inputs.at[position % 2]
    has_next = position + 1 < micro_count
    next_micro = scalars[2 + jnp.minimum(position + 1, micro_count - 1)]
    following = pltpu.make_async_copy(x_hbm.at[0, next_micro], inputs.at[(position + 1) % 2], sems[2])

    @pl.when(has_next)
    def _():
        following.start()

    @pl.when(is_last)
    def _():
        own_copy.start()

    exclude_keys(count, queries, keys)
    normalize(position, x_buf, gain, inv_std, rows_hidden, unit_rows, inv_rows)
    for part in range(3):
        if before_part is not None:
            before_part(part)
        project(position, part, w_qkv, packed, values, queries, keys, rows_hidden)
        if part == 0:
            normed[position] = unit_rows[...].T
        if part == 1:
            hidden[position] = rows_hidden[...].T
    attend(position, packed, probs, attn, queries, keys, scores, halves)

    @pl.when(is_last)
    def _():
        own_copy.wait()
        turned = g_buf[...].T
        ids = lax.broadcasted_iota(jnp.int32, turned.shape, 1)
        masked[position] = jnp.where(ids < count, turned.astype(F32), 0.0).astype(BF)

    @pl.when(has_next)
    def _():
        following.wait()


def recompute_body(slot, sections, scalars, x_hbm, own, gain, w_qkv, *refs):
    micro_count = refs[-22].shape[0]
    position = slot + scalars[1] % 2

    @pl.when(position < micro_count)
    def _():
        recompute_at(position, sections, scalars, x_hbm, own, gain, w_qkv, refs)


def first_body(sections, scalars, x_hbm, own, gain_hbm, wq_hbm, wo_hbm, *refs):
    wq, wo_t, gain_t, gain_row = refs[:4]
    inputs = refs[-16]
    wo, part_sems = refs[-2:]
    micro_count = own.shape[0]
    width = HEADS * HDIM
    parts = []
    for part in range(3):
        cols = pl.ds(part * width, width)
        parts.append(pltpu.make_async_copy(wq_hbm.at[0, :, cols], wq.at[:, cols], part_sems.at[part]))
    parts.append(pltpu.make_async_copy(wo_hbm.at[0], wo, part_sems.at[3]))
    gain_copy = pltpu.make_async_copy(gain_hbm, gain_row, part_sems.at[4])
    x_copy = pltpu.make_async_copy(x_hbm.at[0, scalars[2]], inputs.at[0], part_sems.at[5])
    gain_copy.start()
    x_copy.start()
    for part in parts:
        part.start()
    gain_copy.wait()
    x_copy.wait()

    def one(position, _):
        def before_part(part):
            @pl.when(position == 0)
            def _():
                parts[part].wait()
                if part == 1:
                    gain_t[...] = jnp.broadcast_to(gain_row[0:1, :], (gain_t.shape[1], gain_row.shape[1])).T
                if part == 2:
                    parts[3].wait()
                    wo_t[...] = wo[...].T

        recompute_at(position, sections, scalars, x_hbm, own, gain_row, wq, refs[4:-2], before_part)
        return 0

    lax.fori_loop(0, jnp.minimum(1 + scalars[1] % 2, micro_count), one, 0)


def heads_backward(position, start, heads, gattn, packed, values, probs, out, offsets, grads, halves):
    def g_rows(h):
        return gattn[pl.ds(pl.multiple_of((start + h) * HDIM, 16), HDIM), :]

    def keep(part, h, value):
        rows = pl.ds(pl.multiple_of(offsets[part] + h * HDIM, 16), HDIM)
        out[rows, :] = value.astype(BF)

    def through_values(h, slot):
        grads[slot][...] = contract(values[position * HEADS + start + h], g_rows(h))

    def through_softmax(h, slot):
        grad_prob = grads[slot][...]
        full = probs[position * HEADS + start + h].astype(F32)
        inner = jnp.sum(full * grad_prob, axis=0, keepdims=True)
        halves[slot][...] = (full * (grad_prob - inner)).astype(BF)

    def through_scores(h, slot):
        grad_s = halves[slot][...]
        keep(0, h, contract(packed[position, head_rows(1, start + h), :], grad_s) * SCALE)
        keep(1, h, contract(packed[position, head_rows(0, start + h), :], grad_s, (1, 1)) * SCALE)
        keep(2, h, contract(g_rows(h), probs[position * HEADS + start + h], (1, 1)))

    staged(heads, through_values, through_softmax, through_scores)


def placing(slot, sections, scalars, micro_count):
    section = scalars[0]
    position = slot - 2 * (sections - 1 - section)
    valid = (position >= 0) & (position < micro_count)
    position = jnp.clip(position, 0, micro_count - 1)
    count = scalars[2 + micro_count + scalars[2 + position]]
    return section, position, valid, count


def take_arriving(sections, section, arriving, position, masked):
    if arriving is not None:

        @pl.when(section != sections - 1)
        def _():
            masked[position] = arriving[...]


def into_heads(wo_t, masked, position, gattn):
    chunk = wo_t.shape[0] // 2

    def some_rows(i, _):
        rows = pl.ds(pl.multiple_of(i * chunk, 16), chunk)
        gattn[rows, :] = contract(wo_t[rows, :], masked[position]).astype(BF)
        return 0

    lax.fori_loop(0, 2, some_rows, 0)


def backward_body(slot, sections, has_arriving, passes, scalars, *refs):
    arriving = None
    if has_arriving:
        arriving, refs = refs[0], refs[1:]
    wq, wo_t, gain_t, packed, values, probs, normed, inv_std = refs[:8]
    if passes:
        passed, refs = refs[-9], (*refs[:-9], *refs[-8:])
    grad_packed, masked, gattn, grad_hidden = refs[-8:-4]
    grads, halves = refs[-4:-2], refs[-2:]
    section, position, valid, count = placing(slot, sections, scalars, masked.shape[0])
    width, slots = masked.shape[1:]

    @pl.when(valid)
    def _():
        take_arriving(sections, section, arriving, position, masked)
        into_heads(wo_t, masked, position, gattn)
        span = HEADS * HDIM
        heads_backward(
            position,
            0,
            HEADS,
            gattn,
            packed,
            values,
            probs,
            grad_packed.at[position],
            (0, span, 2 * span),
            grads,
            halves,
        )

    if not passes:
        return

    @pl.when(valid & (section > 0))
    def _():
        chunk = width // WIDTH_CHUNKS

        def some_width(i, carry):
            total, along = carry
            rows = pl.ds(pl.multiple_of(i * chunk, 16), chunk)
            got = contract(wq[rows, :], grad_packed[position]) * over_lanes(gain_t[rows, :], slots)
            grad_hidden[rows, :] = got
            unit = normed[position, rows, :].astype(F32)
            total = total + jnp.sum(got, axis=0, keepdims=True)
            along = along + jnp.sum(got * unit, axis=0, keepdims=True)
            return total, along

        zero = jnp.zeros((1, slots), F32)
        total, along = lax.fori_loop(0, WIDTH_CHUNKS, some_width, (zero, zero))
        mean = total * (1.0 / width)
        along = along * (1.0 / width)
        shown = lax.broadcasted_iota(jnp.int32, (1, slots), 1) < count
        inv = jnp.where(shown, inv_std[position, 0:1, :], 0.0)

        def finish(i, _):
            rows = pl.ds(pl.multiple_of(i * chunk, 16), chunk)
            unit = normed[position, rows, :].astype(F32)
            grad_ln = inv * (grad_hidden[rows, :] - mean - unit * along)
            passed[rows, :] = (masked[position, rows, :].astype(F32) + grad_ln).astype(BF)
            return 0

        lax.fori_loop(0, WIDTH_CHUNKS, finish, 0)


def piece_rows(half):
    return half * PIECES[0] * HDIM, PIECES[half] * HDIM


def gather_half(source, half, compact):
    width = HEADS * HDIM
    start, span = piece_rows(half)
    for part in range(3):
        at = part * width + start
        compact[part * span : (part + 1) * span, :] = source[at : at + span, :]


def weights_body(index, early, sections, scalars, *refs):
    ahead = (scalars[0] == sections - 1) & (scalars[1] % 2 == 1)

    @pl.when(ahead if early else jnp.logical_not(ahead))
    def _():
        weights_at(index, *refs)


def weights_at(index, hidden, attn, grad_packed, masked, *refs):
    compact = refs[-2:]
    acc_qkv, acc_out = refs[-5:-3], refs[-3]
    width = hidden.shape[1]
    chunk = width // 5

    def some_width(i, _):
        rows = pl.ds(pl.multiple_of(i * chunk, 16), chunk)
        for half in range(2):
            total = contract(hidden[index, rows, :], compact[half][...], (1, 1))
            if index > 0:
                total = total + acc_qkv[half][rows, :].astype(F32)
            acc_qkv[half][rows, :] = total.astype(BF)
        total = contract(masked[index, rows, :], attn[index], (1, 1))
        if index > 0:
            total = total + acc_out[rows, :].astype(F32)
        acc_out[rows, :] = total.astype(BF)
        return 0

    for half in range(2):
        gather_half(grad_packed.at[index], half, compact[half])
    lax.fori_loop(0, 5, some_width, 0)


def blocks_out(dp_index, left, right, acc, sent, kept):
    count, block = sent.shape[:2]

    def one(j, target, to):
        at = pl.multiple_of((dp_index ^ j) * block, 16)
        value = contract(left[pl.ds(at, block), :], right[...], (1, 1)) + acc[pl.ds(at, block), :].astype(F32)
        target[to] = value.astype(BF)

    def two(i, _):
        one(2 * i + 1, sent, i)
        one(2 * i, kept, i)
        return 0

    lax.fori_loop(0, count, two, 0)


def tail_out_body(scalars, masked, attn, acc_out, sent, kept):
    last = masked.shape[0] - 1
    blocks_out(scalars[1], masked.at[last], attn.at[last], acc_out, sent, kept)


def tail_half_body(slot, sections, half, has_arriving, scalars, *refs):
    arriving = None
    if has_arriving:
        arriving, refs = refs[0], refs[1:]
    wo_t, packed, values, probs, masked_in, hidden, acc_qkv, gp_all = refs[:8]
    sent, kept = refs[-8 - (half == 0)], refs[-7 - (half == 0)]
    masked = refs[-7] if half == 0 else masked_in
    gattn, compact = refs[-6:-4]
    grads, halves = refs[-4:-2], refs[-2:]
    section, position, valid, _ = placing(slot, sections, scalars, masked.shape[0])
    last = masked.shape[0] - 1
    start, span = piece_rows(half)

    @pl.when(valid)
    def _():
        if half == 0:
            take_arriving(sections, section, arriving, position, masked)
        rows = slice(start, start + span)
        gattn[rows, :] = contract(wo_t[rows, :], masked[position]).astype(BF)
        heads_backward(
            position,
            half * PIECES[0],
            PIECES[half],
            gattn,
            packed,
            values,
            probs,
            compact,
            (0, span, 2 * span),
            grads,
            halves,
        )

    @pl.when(jnp.logical_not(valid))
    def _():
        gather_half(gp_all.at[last], half, compact)

    blocks_out(scalars[1], hidden.at[last], compact, acc_qkv, sent, kept)


def halve_out_body(split, keeps, sends, kept, arrived, *outs):
    for piece, cols in enumerate((slice(0, split), slice(split, kept.shape[2]))):
        kept_out, sent_out = outs[2 * piece : 2 * piece + 2]
        for target, sources in ((kept_out, keeps[piece]), (sent_out, sends[piece])):
            for j, source in enumerate(sources):
                target[j] = (kept[source, :, cols].astype(F32) + arrived[source, :, cols].astype(F32)).astype(BF)


def halve_body(keeps, sends, kept, arrived, kept_out, sent_out):
    for j, source in enumerate(keeps):
        kept_out[j] = (kept[source].astype(F32) + arrived[source].astype(F32)).astype(BF)
    for j, source in enumerate(sends):
        sent_out[j] = (kept[source].astype(F32) + arrived[source].astype(F32)).astype(BF)


def finish_body(split, *refs):
    qkv, out = refs[-2:]
    width = HEADS * HDIM
    for half in range(2):
        start, span = piece_rows(half)
        kept, arrived = refs[2 * half : 2 * half + 2]
        total = kept[0].astype(F32) + arrived[0].astype(F32)
        for part in range(3):
            at = part * width + start
            qkv[:, at : at + span] = total[:, part * span : (part + 1) * span]
    for piece, cols in enumerate((slice(0, split), slice(split, out.shape[1]))):
        kept, arrived = refs[4 + 2 * piece : 6 + 2 * piece]
        out[:, cols] = kept[0].astype(F32) + arrived[0].astype(F32)


def kept_on_chip(shape, dtype):
    return pltpu.VMEM(shape, dtype)


def per_device(activations, cotangent, counts, arrival, norm_gain, qkv_weight, out_weight):
    sections = lax.axis_size("section")
    dp_count = lax.axis_size("dp")
    section = lax.axis_index("section")
    dp_index = lax.axis_index("dp")
    micro_count, slots, width = cotangent.shape
    packed_width = qkv_weight.shape[2]
    head_width = out_weight.shape[2]
    spans = [3 * heads * HDIM for heads in PIECES]
    block = width // dp_count
    activations, cotangent, norm_gain, qkv_weight, out_weight = (
        pltpu.with_memory_space_constraint(x, pltpu.HBM)
        for x in (activations, cotangent, norm_gain, qkv_weight, out_weight)
    )
    scalars = jnp.concatenate([jnp.stack([section, dp_index]).astype(jnp.int32), arrival, counts[:, 0]])

    shapes = {
        "packed": kept_on_chip((micro_count, packed_width, slots), BF),
        "values": kept_on_chip((micro_count * HEADS, slots, HDIM), BF),
        "probs": kept_on_chip((micro_count * HEADS, slots, slots), BF),
        "normed": kept_on_chip((micro_count, width, slots), BF),
        "hidden": kept_on_chip((micro_count, width, slots), BF),
        "attn": kept_on_chip((micro_count, head_width, slots), BF),
        "inv_std": kept_on_chip((micro_count, 8, slots), F32),
        "grad_packed": kept_on_chip((micro_count, packed_width, slots), BF),
        "inputs": kept_on_chip((2, slots, width), BF),
        "masked": kept_on_chip((micro_count, width, slots), BF),
    }
    head_scratch = [pltpu.VMEM((slots, slots), F32)] * 2 + [pltpu.VMEM((slots, slots), BF)] * 2
    row_scratch = [
        pltpu.VMEM((slots, width), BF),
        pltpu.VMEM((slots, width), BF),
        pltpu.VMEM((slots, 128), F32),
        pltpu.VMEM((HEADS, HDIM + 16, slots), BF),
        pltpu.VMEM((HEADS, slots, HDIM + 16), BF),
        pltpu.VMEM((slots, width), BF),
        *head_scratch,
        pltpu.SemaphoreType.DMA,
        pltpu.SemaphoreType.DMA,
        pltpu.SemaphoreType.DMA,
    ]
    state = {}

    def recompute_first():
        outs = tuple(shapes[name] for name in RECOMPUTED)
        results = pl.pallas_call(
            functools.partial(first_body, sections),
            out_shape=(
                kept_on_chip(qkv_weight.shape[1:], BF),
                kept_on_chip((head_width, width), BF),
                kept_on_chip((width, 128), F32),
                kept_on_chip(norm_gain.shape, F32),
                *outs,
            ),
            in_specs=[SMEM, HBM, HBM, HBM, HBM, HBM],
            out_specs=(VMEM,) * (4 + len(outs)),
            scratch_shapes=row_scratch + [pltpu.VMEM((width, head_width), BF), pltpu.SemaphoreType.DMA((6,))],
            compiler_params=pltpu.CompilerParams(vmem_limit_bytes=SCRATCH["recompute_first"] << 10),
            name="recompute_first",
        )(scalars, activations, cotangent, norm_gain, qkv_weight, out_weight)
        state.update(zip(RECOMPUTED, results[4:]))
        return results[:3], results[3]

    def recompute(slot, gain, weights):
        outs = tuple(shapes[name] for name in RECOMPUTED)
        results = pl.pallas_call(
            functools.partial(recompute_body, slot, sections),
            out_shape=outs,
            in_specs=[SMEM, HBM, HBM, VMEM, VMEM] + [ANY] * len(outs),
            out_specs=(VMEM,) * len(outs),
            scratch_shapes=row_scratch,
            input_output_aliases={5 + i: i for i in range(len(outs))},
            compiler_params=pltpu.CompilerParams(vmem_limit_bytes=SCRATCH["recompute"] << 10),
            name="recompute",
        )(scalars, activations, cotangent, gain, weights[0], *(state[name] for name in RECOMPUTED))
        state.update(zip(RECOMPUTED, results))

    def backward(slot, arriving, weights, passes):
        extra = [] if arriving is None else [arriving]
        outs = tuple(shapes[name] for name in COTANGENTS)
        if passes:
            outs = (jax.ShapeDtypeStruct((width, slots), BF), *outs)
        operands = [scalars, *extra, *weights]
        operands += [state[name] for name in ("packed", "values", "probs", "normed", "inv_std")]
        specs = [SMEM] + [VMEM] * (len(operands) - 1)
        given = [name for name in COTANGENTS if name in state]
        aliases = {len(operands) + i: passes + COTANGENTS.index(name) for i, name in enumerate(given)}
        operands += [state[name] for name in given]
        specs += [ANY] * len(given)
        results = pl.pallas_call(
            functools.partial(backward_body, slot, sections, arriving is not None, passes),
            out_shape=outs,
            in_specs=specs,
            out_specs=(VMEM,) * len(outs),
            scratch_shapes=[
                pltpu.VMEM((head_width, slots), BF),
                pltpu.VMEM((width, slots), F32),
                *head_scratch,
            ],
            input_output_aliases=aliases,
            compiler_params=pltpu.CompilerParams(vmem_limit_bytes=SCRATCH["backward"] << 10),
            name="backward",
        )(*operands)
        state.update(zip(COTANGENTS, results[-2:]))
        return results[0]

    def weights_step(index, early):
        operands = [scalars, *(state[name] for name in ("hidden", "attn", "grad_packed", "masked"))]
        specs = [SMEM] + [VMEM] * (len(operands) - 1)
        aliases = {}
        if "sums" in state:
            aliases = {len(operands) + i: i for i in range(3)}
            operands += state["sums"]
            specs += [ANY] * 3
        state["sums"] = pl.pallas_call(
            functools.partial(weights_body, index, early, sections),
            out_shape=(
                *(kept_on_chip((width, span), BF) for span in spans),
                kept_on_chip((width, head_width), BF),
            ),
            in_specs=specs,
            out_specs=(VMEM,) * 3,
            scratch_shapes=[pltpu.VMEM((span, slots), BF) for span in spans],
            input_output_aliases=aliases,
            compiler_params=pltpu.CompilerParams(vmem_limit_bytes=SCRATCH["weights"] << 10),
            name="weights",
        )(*operands)

    def exchange(value, bit):
        pairs = [(source, source ^ bit) for source in range(dp_count)]
        return lax.ppermute(value, "dp", pairs)

    def halve(kept, arrived, bit, held):
        keeps = [i for i, j in enumerate(held) if not j & bit]
        sends = [i for i, j in enumerate(held) if j & bit]
        shape = (len(keeps), *kept.shape[1:])
        kept, sent = pl.pallas_call(
            functools.partial(halve_body, keeps, sends),
            out_shape=(jax.ShapeDtypeStruct(shape, BF), jax.ShapeDtypeStruct(shape, BF)),
            in_specs=[VMEM, VMEM],
            out_specs=(VMEM, VMEM),
            compiler_params=pltpu.CompilerParams(vmem_limit_bytes=SCRATCH["halve"] << 10),
            name="halve",
        )(kept, arrived)
        return kept, exchange(sent, bit), [held[i] for i in keeps]

    last_slot = micro_count + 2 * (sections - 1) - 1
    in_flight = {}
    weights, gain = recompute_first()
    for slot in range(last_slot):
        if 0 < slot < micro_count:
            recompute(slot, gain, weights)
        if slot == micro_count - 1:
            for index in range(micro_count - 1):
                weights_step(index, True)
        pairs = [
            (s, s - 1)
            for s in range(1, sections)
            if 0 <= slot - 2 * (sections - 1 - s) < micro_count
        ]
        passed = backward(slot, in_flight.pop(slot, None), weights, bool(pairs))
        if pairs:
            in_flight[slot + 2] = lax.ppermute(passed, "section", pairs)
        index = slot - 2 * (sections - 1)
        if 0 <= index < micro_count - 1:
            weights_step(index, False)

    arriving = in_flight.pop(last_slot, None)
    pair_shape = (dp_count // 2, block)

    def tail_half(half, scalars, masked, arriving):
        extra = [] if arriving is None else [arriving]
        pair = jax.ShapeDtypeStruct((*pair_shape, spans[half]), BF)
        operands = [scalars, *extra, weights[1], state["packed"], state["values"], state["probs"], masked]
        at_masked = len(operands) - 1
        operands += [state["hidden"], state["sums"][half], state["grad_packed"]]
        specs = [SMEM] + [VMEM] * (len(operands) - 1)
        if half == 0:
            specs[at_masked] = ANY
        results = pl.pallas_call(
            functools.partial(tail_half_body, last_slot, sections, half, arriving is not None),
            out_shape=(pair, pair, shapes["masked"]) if half == 0 else (pair, pair),
            in_specs=specs,
            out_specs=(VMEM,) * (3 if half == 0 else 2),
            scratch_shapes=[pltpu.VMEM((head_width, slots), BF), pltpu.VMEM((spans[half], slots), BF), *head_scratch],
            input_output_aliases={at_masked: 2} if half == 0 else {},
            compiler_params=pltpu.CompilerParams(vmem_limit_bytes=SCRATCH["tail_qkv"] << 10),
            name="tail_qkv",
        )(*operands)
        return results[1], exchange(results[0], 1), (results[2] if half == 0 else masked)

    bits = [1 << i for i in range(1, dp_count.bit_length() - 1)]
    held = list(range(0, dp_count, 2))
    split = head_width // 256 * 128
    orders = [bits, bits[::-1]]
    kept, arrived, masked = tail_half(0, scalars, state["masked"], arriving)
    sent_out, kept_out = pl.pallas_call(
        tail_out_body,
        out_shape=(jax.ShapeDtypeStruct((*pair_shape, head_width), BF),) * 2,
        in_specs=[SMEM] + [VMEM] * 3,
        out_specs=(VMEM, VMEM),
        compiler_params=pltpu.CompilerParams(vmem_limit_bytes=SCRATCH["tail_out"] << 10),
        name="tail_out",
    )(scalars, masked, state["attn"], state["sums"][2])
    arrived_out = exchange(sent_out, 1)
    kept, kept_out = lax.optimization_barrier((kept, kept_out))
    first = halve(kept, arrived, orders[0][0], held)
    later_scalars, first_kept = lax.optimization_barrier((scalars, first[0]))
    first = (first_kept, *first[1:])
    kept, arrived, _ = tail_half(1, later_scalars, masked, None)
    keeps = [[i for i, j in enumerate(held) if not j & bit] for bit in (bits[0], bits[-1])]
    sends = [[i for i, j in enumerate(held) if j & bit] for bit in (bits[0], bits[-1])]
    piece_shapes = [
        jax.ShapeDtypeStruct((len(held) // 2, block, cols), BF)
        for cols in (split, split, head_width - split, head_width - split)
    ]
    kept, kept_out = lax.optimization_barrier((kept, kept_out))
    kept_a, sent_a, kept_b, sent_b = pl.pallas_call(
        functools.partial(halve_out_body, split, keeps, sends),
        out_shape=tuple(piece_shapes),
        in_specs=[VMEM, VMEM],
        out_specs=(VMEM,) * 4,
        compiler_params=pltpu.CompilerParams(vmem_limit_bytes=SCRATCH["halve_out"] << 10),
        name="halve_out",
    )(kept_out, arrived_out)
    out_streams = [
        (kept_a, exchange(sent_a, bits[0]), [held[i] for i in keeps[0]]),
        (kept_b, exchange(sent_b, bits[-1]), [held[i] for i in keeps[1]]),
    ]
    second = halve(kept, arrived, orders[1][0], held)
    qkv_streams = [first, second]
    for step in range(1, len(bits)):
        for i in range(2):
            out_streams[i] = halve(*out_streams[i][:2], orders[i][step], out_streams[i][2])
        waited = lax.optimization_barrier((qkv_streams[0][0], out_streams[0][0], out_streams[1][0]))
        qkv_streams[0] = (waited[0], *qkv_streams[0][1:])
        out_streams = [(waited[1 + i], *out_streams[i][1:]) for i in range(2)]
        for i in range(2):
            qkv_streams[i] = halve(*qkv_streams[i][:2], orders[i][step], qkv_streams[i][2])
    flat = [x for kept, arrived, _ in qkv_streams + out_streams for x in (kept, arrived)]
    qkv_share, out_share = pl.pallas_call(
        functools.partial(finish_body, split),
        out_shape=(
            jax.ShapeDtypeStruct((block, packed_width), F32),
            jax.ShapeDtypeStruct((block, head_width), F32),
        ),
        in_specs=[VMEM] * len(flat),
        out_specs=(VMEM, VMEM),
        compiler_params=pltpu.CompilerParams(vmem_limit_bytes=SCRATCH["finish"] << 10),
        name="finish",
    )(*flat)
    return (qkv_share[None], out_share[None])


def solution(mesh):
    placed = (
        P("section", None, "dp", None),
        P(None, "dp", None),
        P(None, "dp"),
        P(),
        P("section", None),
        P("section", None, None),
        P("section", None, None),
    )
    return jax.shard_map(
        per_device,
        mesh=mesh,
        in_specs=placed,
        out_specs=(P("section", "dp", None), P("section", "dp", None)),
        check_vma=False,
    )
```

```python
import functools

import jax
import jax.numpy as jnp
from jax import lax
from jax.experimental import pallas as pl
from jax.experimental.pallas import tpu as pltpu
from jax.sharding import PartitionSpec as P


HDIM = 80
HEADS = 8
EPSILON = 1e-06
SCALE = HDIM ** (-0.5)
LOG2_E = 1.4426950408889634
PIECES = (HEADS // 2 + 1, HEADS // 2 - 1)
ROWS_AT_A_TIME = 128
WIDTH_CHUNKS = 2

BF = jnp.bfloat16
F32 = jnp.float32
VMEM = pl.BlockSpec(memory_space=pltpu.VMEM)
SMEM = pl.BlockSpec(memory_space=pltpu.SMEM)
ANY = pl.BlockSpec(memory_space=pl.ANY)
HBM = pl.BlockSpec(memory_space=pltpu.HBM)
SCRATCH = {
    "recompute_first": 8192,
    "recompute": 6144,
    "backward": 7168,
    "weights": 3072,
    "tail_out": 3072,
    "tail_qkv": 3072,
    "halve_out": 3072,
    "halve": 3072,
    "finish": 3072,
}

RECOMPUTED = ("packed", "values", "probs", "normed", "hidden", "attn", "inv_std", "masked", "inputs")
COTANGENTS = ("grad_packed", "masked")


def contract(left, right, dims=(1, 0)):
    return lax.dot_general(left, right, ((dims[:1], dims[1:]), ((), ())), preferred_element_type=F32)


def head_rows(part, h):
    return pl.ds(pl.multiple_of(part * (HEADS * HDIM) + h * HDIM, 16), HDIM)


def staged(heads, first, second, third):
    first(0, 0)
    first(1, 1)
    second(0, 0)

    def two_steps(i, _):
        h = 2 * i
        third(h, 0)
        second(h + 1, 1)
        first(h + 2, 0)
        third(h + 1, 1)
        second(h + 2, 0)
        first(h + 3, 1)
        return 0

    lax.fori_loop(0, (heads - 2) // 2, two_steps, 0)
    final = heads - 1
    if heads % 2:
        third(final - 2, 0)
        second(final - 1, 1)
        first(final, 0)
    second(final, final % 2)
    third(final - 1, 1 - final % 2)
    third(final, final % 2)


def over_lanes(column, lanes):
    return jnp.concatenate([column] * (lanes // column.shape[1]), axis=1)


def normalize(position, x_buf, gain, inv_std, rows_hidden, unit_rows, inv_rows):
    slots = x_buf.shape[0]

    def some_rows(i, _):
        rows = pl.ds(pl.multiple_of(i * ROWS_AT_A_TIME, ROWS_AT_A_TIME), ROWS_AT_A_TIME)
        floats = x_buf[rows, :].astype(F32)
        centered = floats - jnp.mean(floats, axis=-1, keepdims=True)
        inv = lax.rsqrt(jnp.mean(centered * centered, axis=-1, keepdims=True) + EPSILON)
        unit = centered * inv
        unit_rows[rows, :] = unit.astype(BF)
        inv_rows[rows, :] = jnp.broadcast_to(inv, (ROWS_AT_A_TIME, inv_rows.shape[1]))
        rows_hidden[rows, :] = (unit * gain[0:1, :]).astype(BF)
        return 0

    lax.fori_loop(0, slots // ROWS_AT_A_TIME, some_rows, 0)
    inv_std[position] = inv_rows[...].T[0:8, :]


def project(position, part, w_qkv, packed, values, queries, keys, rows_hidden):
    width = HEADS * HDIM
    got = contract(rows_hidden[...], w_qkv[:, part * width : (part + 1) * width]).astype(BF)
    turned = got.T
    packed[position, part * width : (part + 1) * width, :] = turned
    for h in range(HEADS):
        cols = slice(h * HDIM, (h + 1) * HDIM)
        if part == 0:
            queries[h, 0:HDIM, :] = turned[cols, :]
        if part == 1:
            keys[h, :, 0:HDIM] = got[:, cols]
        if part == 2:
            values[position * HEADS + h] = got[:, cols]


def exclude_keys(count, queries, keys):
    extra = queries.shape[1] - HDIM
    slots = keys.shape[1]
    ones = lax.broadcasted_iota(jnp.int32, (extra, slots), 0) == 0
    ones = jnp.where(ones, 1.0, 0.0).astype(BF)
    past = (lax.broadcasted_iota(jnp.int32, (slots, extra), 0) >= count) & (
        lax.broadcasted_iota(jnp.int32, (slots, extra), 1) == 0
    )
    low = jnp.where(past, -1e30, 0.0).astype(BF)
    for h in range(HEADS):
        queries[h, HDIM:, :] = ones
        keys[h, :, HDIM:] = low


def attend(position, packed, probs, attn, queries, keys, scores, halves):
    def score(h, slot):
        scores[slot][...] = contract(keys[h], queries[h])

    def soften(h, slot):
        raw = scores[slot][...]
        raised = jnp.exp2((raw - jnp.max(raw, axis=0, keepdims=True)) * (SCALE * LOG2_E))
        prob = (raised * (1.0 / jnp.sum(raised, axis=0, keepdims=True))).astype(BF)
        probs[position * HEADS + h] = prob
        halves[slot][...] = prob

    def mix(h, slot):
        attn[position, head_rows(0, h), :] = contract(packed[position, head_rows(2, h), :], halves[slot][...]).astype(BF)

    staged(HEADS, score, soften, mix)


def recompute_at(position, sections, scalars, x_hbm, own, gain, w_qkv, refs, before_part=None):
    packed, values, probs, normed, hidden, attn, inv_std, masked, inputs = refs[-22:-13]
    rows_hidden, unit_rows, inv_rows, queries, keys, g_buf = refs[-13:-7]
    scores, halves, sems = refs[-7:-5], refs[-5:-3], refs[-3:]
    micro_count = packed.shape[0]
    micro = scalars[2 + position]
    count = scalars[2 + micro_count + micro]
    is_last = scalars[0] == sections - 1
    own_copy = pltpu.make_async_copy(own.at[position], g_buf, sems[1])
    x_buf = inputs.at[position % 2]
    has_next = position + 1 < micro_count
    next_micro = scalars[2 + jnp.minimum(position + 1, micro_count - 1)]
    following = pltpu.make_async_copy(x_hbm.at[0, next_micro], inputs.at[(position + 1) % 2], sems[2])

    @pl.when(has_next)
    def _():
        following.start()

    @pl.when(is_last)
    def _():
        own_copy.start()

    exclude_keys(count, queries, keys)
    normalize(position, x_buf, gain, inv_std, rows_hidden, unit_rows, inv_rows)
    for part in range(3):
        if before_part is not None:
            before_part(part)
        project(position, part, w_qkv, packed, values, queries, keys, rows_hidden)
        if part == 0:
            normed[position] = unit_rows[...].T
        if part == 1:
            hidden[position] = rows_hidden[...].T
    attend(position, packed, probs, attn, queries, keys, scores, halves)

    @pl.when(is_last)
    def _():
        own_copy.wait()
        turned = g_buf[...].T
        ids = lax.broadcasted_iota(jnp.int32, turned.shape, 1)
        masked[position] = jnp.where(ids < count, turned.astype(F32), 0.0).astype(BF)

    @pl.when(has_next)
    def _():
        following.wait()


def runs_ahead(scalars):
    return 1 - scalars[1] % 2


def recompute_body(slot, sections, scalars, x_hbm, own, gain, w_qkv, *refs):
    micro_count = refs[-22].shape[0]
    position = slot + runs_ahead(scalars)

    @pl.when(position < micro_count)
    def _():
        recompute_at(position, sections, scalars, x_hbm, own, gain, w_qkv, refs)


def first_body(sections, scalars, x_hbm, own, gain_hbm, wq_hbm, wo_hbm, *refs):
    wq, wo_t, gain_t, gain_row = refs[:4]
    inputs = refs[-16]
    wo, part_sems = refs[-2:]
    micro_count = own.shape[0]
    width = HEADS * HDIM
    parts = []
    for part in range(3):
        cols = pl.ds(part * width, width)
        parts.append(pltpu.make_async_copy(wq_hbm.at[0, :, cols], wq.at[:, cols], part_sems.at[part]))
    parts.append(pltpu.make_async_copy(wo_hbm.at[0], wo, part_sems.at[3]))
    gain_copy = pltpu.make_async_copy(gain_hbm, gain_row, part_sems.at[4])
    x_copy = pltpu.make_async_copy(x_hbm.at[0, scalars[2]], inputs.at[0], part_sems.at[5])
    gain_copy.start()
    x_copy.start()
    for part in parts:
        part.start()
    gain_copy.wait()
    x_copy.wait()

    def one(position, _):
        def before_part(part):
            @pl.when(position == 0)
            def _():
                parts[part].wait()
                if part == 1:
                    gain_t[...] = jnp.broadcast_to(gain_row[0:1, :], (gain_t.shape[1], gain_row.shape[1])).T
                if part == 2:
                    parts[3].wait()
                    wo_t[...] = wo[...].T

        recompute_at(position, sections, scalars, x_hbm, own, gain_row, wq, refs[4:-2], before_part)
        return 0

    lax.fori_loop(0, jnp.minimum(1 + runs_ahead(scalars), micro_count), one, 0)


def heads_backward(position, start, heads, gattn, packed, values, probs, out, offsets, grads, halves):
    def g_rows(h):
        return gattn[pl.ds(pl.multiple_of((start + h) * HDIM, 16), HDIM), :]

    def keep(part, h, value):
        rows = pl.ds(pl.multiple_of(offsets[part] + h * HDIM, 16), HDIM)
        out[rows, :] = value.astype(BF)

    def through_values(h, slot):
        grads[slot][...] = contract(values[position * HEADS + start + h], g_rows(h))

    def through_softmax(h, slot):
        grad_prob = grads[slot][...]
        full = probs[position * HEADS + start + h].astype(F32)
        inner = jnp.sum(full * grad_prob, axis=0, keepdims=True)
        halves[slot][...] = (full * (grad_prob - inner)).astype(BF)

    def through_scores(h, slot):
        grad_s = halves[slot][...]
        keep(0, h, contract(packed[position, head_rows(1, start + h), :], grad_s) * SCALE)
        keep(1, h, contract(packed[position, head_rows(0, start + h), :], grad_s, (1, 1)) * SCALE)
        keep(2, h, contract(g_rows(h), probs[position * HEADS + start + h], (1, 1)))

    staged(heads, through_values, through_softmax, through_scores)


def placing(slot, sections, scalars, micro_count):
    section = scalars[0]
    position = slot - 2 * (sections - 1 - section)
    valid = (position >= 0) & (position < micro_count)
    position = jnp.clip(position, 0, micro_count - 1)
    count = scalars[2 + micro_count + scalars[2 + position]]
    return section, position, valid, count


def take_arriving(sections, section, arriving, position, masked):
    if arriving is not None:

        @pl.when(section != sections - 1)
        def _():
            masked[position] = arriving[...]


def into_heads(wo_t, masked, position, gattn):
    chunk = wo_t.shape[0] // 4

    def some_rows(i, _):
        rows = pl.ds(pl.multiple_of(i * chunk, 16), chunk)
        gattn[rows, :] = contract(wo_t[rows, :], masked[position]).astype(BF)
        return 0

    lax.fori_loop(0, 4, some_rows, 0)


def backward_body(slot, sections, has_arriving, passes, scalars, *refs):
    arriving = None
    if has_arriving:
        arriving, refs = refs[0], refs[1:]
    wq, wo_t, gain_t, packed, values, probs, normed, inv_std = refs[:8]
    if passes:
        passed, refs = refs[-9], (*refs[:-9], *refs[-8:])
    grad_packed, masked, gattn, grad_hidden = refs[-8:-4]
    grads, halves = refs[-4:-2], refs[-2:]
    section, position, valid, count = placing(slot, sections, scalars, masked.shape[0])
    width, slots = masked.shape[1:]

    @pl.when(valid)
    def _():
        take_arriving(sections, section, arriving, position, masked)
        into_heads(wo_t, masked, position, gattn)
        span = HEADS * HDIM
        heads_backward(
            position,
            0,
            HEADS,
            gattn,
            packed,
            values,
            probs,
            grad_packed.at[position],
            (0, span, 2 * span),
            grads,
            halves,
        )

    if not passes:
        return

    @pl.when(valid & (section > 0))
    def _():
        chunk = width // WIDTH_CHUNKS

        def some_width(i, carry):
            total, along = carry
            rows = pl.ds(pl.multiple_of(i * chunk, 16), chunk)
            got = contract(wq[rows, :], grad_packed[position]) * over_lanes(gain_t[rows, :], slots)
            grad_hidden[rows, :] = got
            unit = normed[position, rows, :].astype(F32)
            total = total + jnp.sum(got, axis=0, keepdims=True)
            along = along + jnp.sum(got * unit, axis=0, keepdims=True)
            return total, along

        zero = jnp.zeros((1, slots), F32)
        total, along = lax.fori_loop(0, WIDTH_CHUNKS, some_width, (zero, zero))
        mean = total * (1.0 / width)
        along = along * (1.0 / width)
        shown = lax.broadcasted_iota(jnp.int32, (1, slots), 1) < count
        inv = jnp.where(shown, inv_std[position, 0:1, :], 0.0)

        piece = width // 5

        def finish(i, _):
            rows = pl.ds(pl.multiple_of(i * piece, 16), piece)
            unit = normed[position, rows, :].astype(F32)
            grad_ln = inv * (grad_hidden[rows, :] - mean - unit * along)
            passed[rows, :] = (masked[position, rows, :].astype(F32) + grad_ln).astype(BF)
            return 0

        lax.fori_loop(0, 5, finish, 0)


def piece_rows(half):
    return half * PIECES[0] * HDIM, PIECES[half] * HDIM


def gather_half(source, half, compact):
    width = HEADS * HDIM
    start, span = piece_rows(half)
    for part in range(3):
        at = part * width + start
        compact[part * span : (part + 1) * span, :] = source[at : at + span, :]


def weights_body(index, hidden, attn, grad_packed, masked, *refs):
    compact = refs[-2:]
    acc_qkv, acc_out = refs[-5:-3], refs[-3]
    width = hidden.shape[1]
    chunk = width // 5

    def some_width(i, _):
        rows = pl.ds(pl.multiple_of(i * chunk, 16), chunk)
        for half in range(2):
            total = contract(hidden[index, rows, :], compact[half][...], (1, 1))
            if index > 0:
                total = total + acc_qkv[half][rows, :].astype(F32)
            acc_qkv[half][rows, :] = total.astype(BF)
        total = contract(masked[index, rows, :], attn[index], (1, 1))
        if index > 0:
            total = total + acc_out[rows, :].astype(F32)
        acc_out[rows, :] = total.astype(BF)
        return 0

    for half in range(2):
        gather_half(grad_packed.at[index], half, compact[half])
    lax.fori_loop(0, 5, some_width, 0)


def blocks_out(dp_index, left, right, acc, sent, kept):
    count, block = sent.shape[:2]

    def one(j, target, to):
        at = pl.multiple_of((dp_index ^ j) * block, 16)
        value = contract(left[pl.ds(at, block), :], right[...], (1, 1)) + acc[pl.ds(at, block), :].astype(F32)
        target[to] = value.astype(BF)

    def two(i, _):
        one(2 * i + 1, sent, i)
        one(2 * i, kept, i)
        return 0

    lax.fori_loop(0, count, two, 0)


def tail_out_body(scalars, masked, attn, acc_out, sent, kept):
    last = masked.shape[0] - 1
    blocks_out(scalars[1], masked.at[last], attn.at[last], acc_out, sent, kept)


def tail_half_body(slot, sections, half, has_arriving, scalars, *refs):
    arriving = None
    if has_arriving:
        arriving, refs = refs[0], refs[1:]
    wo_t, packed, values, probs, masked_in, hidden, acc_qkv, gp_all = refs[:8]
    sent, kept = refs[-8 - (half == 0)], refs[-7 - (half == 0)]
    masked = refs[-7] if half == 0 else masked_in
    gattn, compact = refs[-6:-4]
    grads, halves = refs[-4:-2], refs[-2:]
    section, position, valid, _ = placing(slot, sections, scalars, masked.shape[0])
    last = masked.shape[0] - 1
    start, span = piece_rows(half)

    @pl.when(valid)
    def _():
        if half == 0:
            take_arriving(sections, section, arriving, position, masked)
        rows = slice(start, start + span)
        gattn[rows, :] = contract(wo_t[rows, :], masked[position]).astype(BF)
        heads_backward(
            position,
            half * PIECES[0],
            PIECES[half],
            gattn,
            packed,
            values,
            probs,
            compact,
            (0, span, 2 * span),
            grads,
            halves,
        )

    @pl.when(jnp.logical_not(valid))
    def _():
        gather_half(gp_all.at[last], half, compact)

    blocks_out(scalars[1], hidden.at[last], compact, acc_qkv, sent, kept)


def halve_body(keeps, sends, kept, arrived, kept_out, sent_out):
    for j, source in enumerate(keeps):
        kept_out[j] = (kept[source].astype(F32) + arrived[source].astype(F32)).astype(BF)
    for j, source in enumerate(sends):
        sent_out[j] = (kept[source].astype(F32) + arrived[source].astype(F32)).astype(BF)


def finish_body(*refs):
    qkv, out = refs[-2:]
    width = HEADS * HDIM
    for half in range(2):
        start, span = piece_rows(half)
        kept, arrived = refs[2 * half : 2 * half + 2]
        total = kept[0].astype(F32) + arrived[0].astype(F32)
        for part in range(3):
            at = part * width + start
            qkv[:, at : at + span] = total[:, part * span : (part + 1) * span]
    kept, arrived = refs[4:6]
    out[...] = kept[0].astype(F32) + arrived[0].astype(F32)


def kept_on_chip(shape, dtype):
    return pltpu.VMEM(shape, dtype)


def per_device(activations, cotangent, counts, arrival, norm_gain, qkv_weight, out_weight):
    sections = lax.axis_size("section")
    dp_count = lax.axis_size("dp")
    section = lax.axis_index("section")
    dp_index = lax.axis_index("dp")
    micro_count, slots, width = cotangent.shape
    packed_width = qkv_weight.shape[2]
    head_width = out_weight.shape[2]
    spans = [3 * heads * HDIM for heads in PIECES]
    block = width // dp_count
    activations, cotangent, norm_gain, qkv_weight, out_weight = (
        pltpu.with_memory_space_constraint(x, pltpu.HBM)
        for x in (activations, cotangent, norm_gain, qkv_weight, out_weight)
    )
    scalars = jnp.concatenate([jnp.stack([section, dp_index]).astype(jnp.int32), arrival, counts[:, 0]])

    shapes = {
        "packed": kept_on_chip((micro_count, packed_width, slots), BF),
        "values": kept_on_chip((micro_count * HEADS, slots, HDIM), BF),
        "probs": kept_on_chip((micro_count * HEADS, slots, slots), BF),
        "normed": kept_on_chip((micro_count, width, slots), BF),
        "hidden": kept_on_chip((micro_count, width, slots), BF),
        "attn": kept_on_chip((micro_count, head_width, slots), BF),
        "inv_std": kept_on_chip((micro_count, 8, slots), F32),
        "grad_packed": kept_on_chip((micro_count, packed_width, slots), BF),
        "inputs": kept_on_chip((2, slots, width), BF),
        "masked": kept_on_chip((micro_count, width, slots), BF),
    }
    head_scratch = [pltpu.VMEM((slots, slots), F32)] * 2 + [pltpu.VMEM((slots, slots), BF)] * 2
    row_scratch = [
        pltpu.VMEM((slots, width), BF),
        pltpu.VMEM((slots, width), BF),
        pltpu.VMEM((slots, 128), F32),
        pltpu.VMEM((HEADS, HDIM + 16, slots), BF),
        pltpu.VMEM((HEADS, slots, HDIM + 16), BF),
        pltpu.VMEM((slots, width), BF),
        *head_scratch,
        pltpu.SemaphoreType.DMA,
        pltpu.SemaphoreType.DMA,
        pltpu.SemaphoreType.DMA,
    ]
    state = {}

    def recompute_first():
        outs = tuple(shapes[name] for name in RECOMPUTED)
        results = pl.pallas_call(
            functools.partial(first_body, sections),
            out_shape=(
                kept_on_chip(qkv_weight.shape[1:], BF),
                kept_on_chip((head_width, width), BF),
                kept_on_chip((width, 128), F32),
                kept_on_chip(norm_gain.shape, F32),
                *outs,
            ),
            in_specs=[SMEM, HBM, HBM, HBM, HBM, HBM],
            out_specs=(VMEM,) * (4 + len(outs)),
            scratch_shapes=row_scratch + [pltpu.VMEM((width, head_width), BF), pltpu.SemaphoreType.DMA((6,))],
            compiler_params=pltpu.CompilerParams(vmem_limit_bytes=SCRATCH["recompute_first"] << 10),
            name="recompute_first",
        )(scalars, activations, cotangent, norm_gain, qkv_weight, out_weight)
        state.update(zip(RECOMPUTED, results[4:]))
        return results[:3], results[3]

    def recompute(slot, gain, weights):
        outs = tuple(shapes[name] for name in RECOMPUTED)
        results = pl.pallas_call(
            functools.partial(recompute_body, slot, sections),
            out_shape=outs,
            in_specs=[SMEM, HBM, HBM, VMEM, VMEM] + [ANY] * len(outs),
            out_specs=(VMEM,) * len(outs),
            scratch_shapes=row_scratch,
            input_output_aliases={5 + i: i for i in range(len(outs))},
            compiler_params=pltpu.CompilerParams(vmem_limit_bytes=SCRATCH["recompute"] << 10),
            name="recompute",
        )(scalars, activations, cotangent, gain, weights[0], *(state[name] for name in RECOMPUTED))
        state.update(zip(RECOMPUTED, results))

    def backward(slot, arriving, weights, passes):
        extra = [] if arriving is None else [arriving]
        outs = tuple(shapes[name] for name in COTANGENTS)
        if passes:
            outs = (jax.ShapeDtypeStruct((width, slots), BF), *outs)
        operands = [scalars, *extra, *weights]
        operands += [state[name] for name in ("packed", "values", "probs", "normed", "inv_std")]
        specs = [SMEM] + [VMEM] * (len(operands) - 1)
        given = [name for name in COTANGENTS if name in state]
        aliases = {len(operands) + i: passes + COTANGENTS.index(name) for i, name in enumerate(given)}
        operands += [state[name] for name in given]
        specs += [ANY] * len(given)
        results = pl.pallas_call(
            functools.partial(backward_body, slot, sections, arriving is not None, passes),
            out_shape=outs,
            in_specs=specs,
            out_specs=(VMEM,) * len(outs),
            scratch_shapes=[
                pltpu.VMEM((head_width, slots), BF),
                pltpu.VMEM((width, slots), F32),
                *head_scratch,
            ],
            input_output_aliases=aliases,
            compiler_params=pltpu.CompilerParams(vmem_limit_bytes=SCRATCH["backward"] << 10),
            name="backward",
        )(*operands)
        state.update(zip(COTANGENTS, results[-2:]))
        return results[0]

    def weights_step(index):
        operands = [state[name] for name in ("hidden", "attn", "grad_packed", "masked")]
        specs = [VMEM] * len(operands)
        aliases = {}
        if "sums" in state:
            aliases = {len(operands) + i: i for i in range(3)}
            operands += state["sums"]
            specs += [ANY] * 3
        state["sums"] = pl.pallas_call(
            functools.partial(weights_body, index),
            out_shape=(
                *(kept_on_chip((width, span), BF) for span in spans),
                kept_on_chip((width, head_width), BF),
            ),
            in_specs=specs,
            out_specs=(VMEM,) * 3,
            scratch_shapes=[pltpu.VMEM((span, slots), BF) for span in spans],
            input_output_aliases=aliases,
            compiler_params=pltpu.CompilerParams(vmem_limit_bytes=SCRATCH["weights"] << 10),
            name="weights",
        )(*operands)

    def exchange(value, bit):
        pairs = [(source, source ^ bit) for source in range(dp_count)]
        return lax.ppermute(value, "dp", pairs)

    def halve(kept, arrived, bit, held):
        keeps = [i for i, j in enumerate(held) if not j & bit]
        sends = [i for i, j in enumerate(held) if j & bit]
        shape = (len(keeps), *kept.shape[1:])
        kept, sent = pl.pallas_call(
            functools.partial(halve_body, keeps, sends),
            out_shape=(jax.ShapeDtypeStruct(shape, BF), jax.ShapeDtypeStruct(shape, BF)),
            in_specs=[VMEM, VMEM],
            out_specs=(VMEM, VMEM),
            compiler_params=pltpu.CompilerParams(vmem_limit_bytes=SCRATCH["halve"] << 10),
            name="halve",
        )(kept, arrived)
        return kept, exchange(sent, bit), [held[i] for i in keeps]

    last_slot = micro_count + 2 * (sections - 1) - 1
    in_flight = {}
    weights, gain = recompute_first()
    for slot in range(last_slot):
        if 0 < slot < micro_count:
            recompute(slot, gain, weights)
        pairs = [
            (s, s - 1)
            for s in range(1, sections)
            if 0 <= slot - 2 * (sections - 1 - s) < micro_count
        ]
        passed = backward(slot, in_flight.pop(slot, None), weights, bool(pairs))
        if pairs:
            in_flight[slot + 2] = lax.ppermute(passed, "section", pairs)
        index = slot - 2 * (sections - 1)
        if 0 <= index < micro_count - 1:
            weights_step(index)

    arriving = in_flight.pop(last_slot, None)
    pair_shape = (dp_count // 2, block)

    def tail_half(half, scalars, masked, arriving):
        extra = [] if arriving is None else [arriving]
        pair = jax.ShapeDtypeStruct((*pair_shape, spans[half]), BF)
        operands = [scalars, *extra, weights[1], state["packed"], state["values"], state["probs"], masked]
        at_masked = len(operands) - 1
        operands += [state["hidden"], state["sums"][half], state["grad_packed"]]
        specs = [SMEM] + [VMEM] * (len(operands) - 1)
        if half == 0:
            specs[at_masked] = ANY
        results = pl.pallas_call(
            functools.partial(tail_half_body, last_slot, sections, half, arriving is not None),
            out_shape=(pair, pair, shapes["masked"]) if half == 0 else (pair, pair),
            in_specs=specs,
            out_specs=(VMEM,) * (3 if half == 0 else 2),
            scratch_shapes=[pltpu.VMEM((head_width, slots), BF), pltpu.VMEM((spans[half], slots), BF), *head_scratch],
            input_output_aliases={at_masked: 2} if half == 0 else {},
            compiler_params=pltpu.CompilerParams(vmem_limit_bytes=SCRATCH["tail_qkv"] << 10),
            name="tail_qkv",
        )(*operands)
        return results[1], exchange(results[0], 1), (results[2] if half == 0 else masked)

    bits = [1 << i for i in range(1, dp_count.bit_length() - 1)]
    held = list(range(0, dp_count, 2))
    orders = [bits, bits[::-1]]
    kept, arrived, masked = tail_half(0, scalars, state["masked"], arriving)
    sent_out, kept_out = pl.pallas_call(
        tail_out_body,
        out_shape=(jax.ShapeDtypeStruct((*pair_shape, head_width), BF),) * 2,
        in_specs=[SMEM] + [VMEM] * 3,
        out_specs=(VMEM, VMEM),
        compiler_params=pltpu.CompilerParams(vmem_limit_bytes=SCRATCH["tail_out"] << 10),
        name="tail_out",
    )(scalars, masked, state["attn"], state["sums"][2])
    arrived_out = exchange(sent_out, 1)
    kept, kept_out = lax.optimization_barrier((kept, kept_out))
    first = halve(kept, arrived, orders[0][0], held)
    kept_out, first_kept = lax.optimization_barrier((kept_out, first[0]))
    third = halve(kept_out, arrived_out, orders[1][0], held)
    later_scalars, third_kept = lax.optimization_barrier((scalars, third[0]))
    first, third = (first_kept, *first[1:]), (third_kept, *third[1:])
    kept, arrived, _ = tail_half(1, later_scalars, masked, None)
    second = halve(kept, arrived, orders[1][0], held)
    streams = [first, second, third]
    for step in range(1, len(bits)):
        streams[2] = halve(*streams[2][:2], orders[1][step], streams[2][2])
        waited = lax.optimization_barrier((streams[0][0], streams[2][0]))
        streams[0] = (waited[0], *streams[0][1:])
        streams[2] = (waited[1], *streams[2][1:])
        streams[0] = halve(*streams[0][:2], orders[0][step], streams[0][2])
        streams[1] = halve(*streams[1][:2], orders[1][step], streams[1][2])
    flat = [x for kept, arrived, _ in streams for x in (kept, arrived)]
    qkv_share, out_share = pl.pallas_call(
        finish_body,
        out_shape=(
            jax.ShapeDtypeStruct((block, packed_width), F32),
            jax.ShapeDtypeStruct((block, head_width), F32),
        ),
        in_specs=[VMEM] * len(flat),
        out_specs=(VMEM, VMEM),
        compiler_params=pltpu.CompilerParams(vmem_limit_bytes=SCRATCH["finish"] << 10),
        name="finish",
    )(*flat)
    return (qkv_share[None], out_share[None])


def solution(mesh):
    placed = (
        P("section", None, "dp", None),
        P(None, "dp", None),
        P(None, "dp"),
        P(),
        P("section", None),
        P("section", None, None),
        P("section", None, None),
    )
    return jax.shard_map(
        per_device,
        mesh=mesh,
        in_specs=placed,
        out_specs=(P("section", "dp", None), P("section", "dp", None)),
        check_vma=False,
    )
```
